32 devices in a mesh: depth: 8 (over y, x, core), plan: 4 (over z).
Axes of the slice: x: 2, y: 2, z: 4, core: 2. Of those that a mesh axis runs over, the one named last changes fastest.
Arguments:
- stress: float32 [6, 64, 64, 256], P(None, 'depth', 'plan'), may hold values from -6 to 6
- velocity: float32 [3, 64, 64, 256], P(None, 'depth', 'plan'), may hold values from -3 to 3
- density: float32 [64, 64, 256], P('depth', 'plan'), may hold values from 1 to 4
- branch_flags: int32 [64, 64, 256], P('depth', 'plan'), may hold values from 0 to 2
- pile_velocity: float32 [3, 49152], P(None, 'depth'), may hold values from -3 to 3
- pile_mass: float32 [49152], P('depth'), may hold values from 0.5 to 2
- jack_force: float32 [3, 49152], P(None, 'depth'), may hold values from -6 to 6
- pair_elem: int32 [8, 8192], P('depth', 'plan'), may hold values from 0 to 18431, as said below
- pair_cell: int32 [8, 8192], P('depth', 'plan'), may hold values from -1 to 32767, as said below
Outputs:
- stress_out: float32 [6, 64, 64, 256], P(None, 'depth', 'plan')
- velocity_out: float32 [3, 64, 64, 256], P(None, 'depth', 'plan')
- pile_velocity_out: float32 [3, 49152], P(None, 'depth')
The draws below stay inside these ranges and needn't reach their ends.
Inputs may be any that keep to these rules, and one draw needn't show every extreme that they name: `pair_elem`: counted from block d - 1 for depth index d, it names an element of the pile: blocks d - 1, d, d + 1 only, never below block 0 or above the last block. `pair_cell`: live pairs (cell >= 0) of one device are its first slots; at most 2048 on one device; all slots live on every device of one depth index, the tip, which lies above the middle depth index and below the last; fewer live on the depth indices before it, none after it.
All inputs are finite; a program needn't handle non-finite values.
Results may differ from the reference program's by a relative error of at most 0.00016.
Values sent between devices are 32-bit elements; how exact they have to be, the bound alone decides.
No kernel may reach another device: no remote copies, remote signals or barrier semaphores. Data moves between devices by JAX's collectives and lax.ppermute only.
A program may use at most 64 MiB of HBM per device.

```python
import math
import jax
import jax.numpy as jnp

CZ = 8
CX = 16
CY = 256
PILE_DEV = 6144
PAIRS_DEV = 2048
STEPS = 3
NZ = 64
NX = 64
PILE = 49152
N_DEPTH = 8
N_PLAN = 4


def tip_layout(key):
    tip_slab = jax.random.randint(jax.random.fold_in(key, 11), (), N_DEPTH // 2 + 1, N_DEPTH - 1)
    row_ids = jnp.arange(N_DEPTH, dtype=jnp.int32)[:, None]
    col_ids = jnp.arange(N_PLAN * PAIRS_DEV, dtype=jnp.int32)[None, :]
    slot_ids = col_ids % PAIRS_DEV
    live_count = jnp.where(row_ids == tip_slab, PAIRS_DEV, jnp.where(row_ids < tip_slab, PAIRS_DEV // 3, 0))
    return (row_ids, slot_ids < live_count)


def draw_pair_elem(key, part):
    row_ids, is_live = tip_layout(key)
    lowest = jnp.where(row_ids == 0, PILE_DEV, 0)
    highest = jnp.where(row_ids == N_DEPTH - 1, 2 * PILE_DEV, 3 * PILE_DEV)
    drawn = jax.random.randint(jax.random.fold_in(key, 12), (N_DEPTH, N_PLAN * PAIRS_DEV), 0, 3 * PILE_DEV)
    return (lowest + drawn % (highest - lowest)).astype(jnp.int32)


def draw_pair_cell(key, part):
    row_ids, is_live = tip_layout(key)
    drawn = jax.random.randint(jax.random.fold_in(key, 13), (N_DEPTH, N_PLAN * PAIRS_DEV), 0, CZ * CX * CY)
    return jnp.where(is_live, drawn, -1).astype(jnp.int32)


def touch_ends(array, own_key, least, high):
    longest = array.shape.index(max(array.shape))
    spots = []
    for shift in (0, 1):
        where = [jax.random.randint(jax.random.fold_in(own_key, axis), (), 0, length) for axis, length in enumerate(array.shape)]
        where[longest] = (where[longest] + shift) % array.shape[longest]
        spots.append(tuple(where))
    return array.at[spots[0]].set(least).at[spots[1]].set(high)


def shard_levels(own_key, extent, shards, smallest, high):
    def one(position, blocks):
        heights = jax.random.uniform(jax.random.fold_in(jax.random.fold_in(own_key, 6), position), (blocks,), jnp.float32, smallest / len(shards), high / len(shards))
        return jnp.repeat(jnp.exp(heights), extent[position] // blocks).reshape((-1,) + (1,) * (len(extent) - position - 1))

    factor_of = one(*shards[0])
    for cut in shards[1:]:
        factor_of = factor_of * one(*cut)
    return factor_of


def scatter_about(rng, dims, scale, most, split=(), held_as=jnp.bfloat16):
    result = jax.random.normal(rng, dims, jnp.float32) * scale
    if len(split) > 0:
        result = shard_levels(rng, dims, split, -0.22, 0.18) * result
    return jnp.clip(result, min=-most, max=most).astype(held_as)


def setup_inputs(seed: int = 0) -> dict:
    arg_keys = jax.random.split(jax.random.key(seed), 10)
    return {
        "stress": scatter_about(arg_keys[0], (6, NZ, NX, CY), 1.0, 6.0, ((1, 8), (2, 4)), jnp.float32),
        "velocity": scatter_about(arg_keys[1], (3, NZ, NX, CY), 0.5, 3.0, ((1, 8), (2, 4)), jnp.float32),
        "density": jnp.clip(jnp.exp(math.log(4.0) - 1.3862944 * jax.random.uniform(arg_keys[2], (NZ, NX, CY), jnp.float32) ** shard_levels(arg_keys[2], (NZ, NX, CY), ((0, 8), (1, 4)), -0.2, 0.2)), 1.0, 4.0),
        "branch_flags": touch_ends(jax.random.randint(arg_keys[3], (NZ, NX, CY), 0, 3), jax.random.fold_in(arg_keys[3], 1), 0, 2).astype(jnp.int32),
        "pile_velocity": scatter_about(arg_keys[4], (3, PILE), 0.5, 3.0, ((1, 8),), jnp.float32),
        "pile_mass": jnp.clip(jnp.exp(math.log(2.0) - 1.3862944 * jax.random.uniform(arg_keys[5], (PILE,), jnp.float32) ** shard_levels(arg_keys[5], (PILE,), ((0, 8),), -0.2, 0.2)), 0.5, 2.0),
        "jack_force": scatter_about(arg_keys[6], (3, PILE), 1.0, 6.0, ((1, 8),), jnp.float32),
        "pair_elem": draw_pair_elem(jax.random.fold_in(arg_keys[9], 71), 0),
        "pair_cell": draw_pair_cell(jax.random.fold_in(arg_keys[9], 71), 0),
    }


time_step = 0.2
penalty = 1.0
lame_first = 1.0
shear_modulus = 1.0
cone_rate = 1.5
symmetric_index = ((0, 3, 4), (3, 1, 5), (4, 5, 2))

def slopes_of(padded):
    along_depth = 0.5 * (padded[:, 2:, 1:-1, 1:-1] - padded[:, :-2, 1:-1, 1:-1])
    along_plan = 0.5 * (padded[:, 1:-1, 2:, 1:-1] - padded[:, 1:-1, :-2, 1:-1])
    along_last = 0.5 * (padded[:, 1:-1, 1:-1, 2:] - padded[:, 1:-1, 1:-1, :-2])
    return (along_depth, along_plan, along_last)

def divergence(padded):
    slopes = slopes_of(padded)
    return jnp.stack([slopes[0][symmetric_index[component][0]] + slopes[1][symmetric_index[component][1]] + slopes[2][symmetric_index[component][2]] for component in range(3)])

def strain_rate(padded):
    slopes = slopes_of(padded)
    return jnp.stack([slopes[0][0], slopes[1][1], slopes[2][2], 0.5 * (slopes[1][0] + slopes[0][1]), 0.5 * (slopes[2][0] + slopes[0][2]), 0.5 * (slopes[2][1] + slopes[1][2])])

def return_map(trial_stress, branch_flags):
    pressure = (trial_stress[0] + trial_stress[1] + trial_stress[2]) / 3.0
    deviator = jnp.stack([trial_stress[0] - pressure, trial_stress[1] - pressure, trial_stress[2] - pressure, trial_stress[3], trial_stress[4], trial_stress[5]])
    second = 0.5 * (deviator[0] * deviator[0] + deviator[1] * deviator[1] + deviator[2] * deviator[2]) + deviator[3] * deviator[3] + deviator[4] * deviator[4] + deviator[5] * deviator[5]
    shrink = 1.0 / (1.0 + cone_rate * jnp.sqrt(second))
    empty_part = jnp.zeros_like(pressure)
    spherical = jnp.stack([pressure, pressure, pressure, empty_part, empty_part, empty_part])
    cone_stress = deviator * shrink + spherical
    return jnp.where(branch_flags == 0, trial_stress, jnp.where(branch_flags == 1, cone_stress, spherical))

def stress_update(stress, padded_velocity, branch_flags):
    strain = strain_rate(padded_velocity)
    increment = 2.0 * shear_modulus * strain
    increment = increment.at[:3].add(lame_first * (strain[0] + strain[1] + strain[2]))
    return return_map(stress + time_step * increment, branch_flags)

def pad_cells(field):
    return jnp.pad(field, ((0, 0), (1, 1), (1, 1), (1, 1)))

def reference(stress, velocity, density, branch_flags, pile_velocity, pile_mass, jack_force, pair_elem, pair_cell):
    row_ids = jnp.arange(N_DEPTH, dtype=jnp.int32)[:, None]
    col_ids = jnp.arange(N_PLAN * PAIRS_DEV, dtype=jnp.int32)[None, :]
    plan_ids = col_ids // PAIRS_DEV
    weight = (pair_cell >= 0).astype(jnp.float32).reshape(-1)
    clamped = jnp.maximum(pair_cell, 0)
    depth_cell = row_ids * CZ + clamped // (CX * CY)
    plan_cell = plan_ids * CX + clamped // CY % CX
    last_cell = clamped % CY
    cell_index = ((depth_cell * NX + plan_cell) * CY + last_cell).reshape(-1).astype(jnp.int32)
    elem_index = jnp.clip((row_ids - 1) * PILE_DEV + pair_elem, 0, PILE - 1).reshape(-1).astype(jnp.int32)
    for step_number in range(STEPS):
        stress_force = divergence(pad_cells(stress))
        flat_velocity = velocity.reshape(3, -1)
        pushes = penalty * (pile_velocity[:, elem_index] - flat_velocity[:, cell_index]) * weight
        on_cells = jnp.zeros_like(flat_velocity).at[:, cell_index].add(pushes).reshape(velocity.shape)
        on_pile = jnp.zeros_like(pile_velocity).at[:, elem_index].add(pushes)
        velocity = velocity + time_step * (stress_force + on_cells) / density
        pile_velocity = pile_velocity + time_step * (jack_force - on_pile) / pile_mass
        stress = stress_update(stress, pad_cells(velocity), branch_flags)
    return (stress, velocity, pile_velocity)
```

```python
import functools

import jax
import jax.numpy as jnp
from jax import lax
from jax.experimental import pallas as pl
from jax.experimental.pallas import tpu as pltpu
from jax.sharding import PartitionSpec as P

STEPS = 3
time_step = 0.2
cone_rate = 1.5
F32, BF16, I32 = jnp.float32, jnp.bfloat16, jnp.int32
COLS = 256
DEPTH_PART = (0, 3, 4)
PLAN_PART = (3, 1, 5)
LAST_PART = (4, 5, 2)


class Sizes:
    def __init__(self, stress, pile_velocity, pair_cell):
        self.cz, self.cx, self.cy = stress.shape[1:]
        self.rows = self.cz * self.cx
        self.pile = pile_velocity.shape[1]
        self.pr = self.pile // COLS
        self.wp = -(-3 * self.pr // 16) * 16
        self.pairs = pair_cell.shape[1]
        self.kn = self.pairs // COLS
        self.nd = lax.axis_size("depth")
        self.np = lax.axis_size("plan")


def partner_b(index, count):
    return jnp.where(
        index % 2 == 0, lax.rem(index + count - 1, count), lax.rem(index + 1, count)
    )


def low_high(index, count, ref_a, ref_b, where):
    a, b = ref_a[where], ref_b[where]
    even = index % 2 == 0
    zero = jnp.zeros_like(a)
    low = jnp.where(index > 0, jnp.where(even, b, a), zero)
    high = jnp.where(index < count - 1, jnp.where(even, a, b), zero)
    return low, high


def split(x):
    high = x.astype(BF16)
    return high, (x - high.astype(F32)).astype(BF16)


def hits(ids, count):
    return lax.broadcasted_iota(I32, (count, ids.shape[1]), 0) == ids


def one_hot(ids, count):
    return jnp.where(hits(ids, count), 1.0, 0.0).astype(BF16)


def gather_chunk(table, row_ids, col_ids, parts, rows):
    pick = one_hot(col_ids, COLS)
    got = jnp.dot(table[0][...], pick, preferred_element_type=F32)
    got = got + jnp.dot(table[1][...], pick, preferred_element_type=F32)
    mask = hits(row_ids, rows)
    return [
        jnp.sum(jnp.where(mask, got[c * rows : (c + 1) * rows], 0.0), axis=0, keepdims=True)
        for c in range(parts)
    ]


def scatter_chunk(values, row_ids, col_ids, rows):
    put = one_hot(col_ids, COLS)
    mask = hits(row_ids, rows)
    total = None
    for piece in zip(*[split(v) for v in values]):
        spread = jnp.concatenate(
            [jnp.where(mask, v.astype(F32), 0.0) for v in piece], axis=0
        ).astype(BF16)
        term = lax.dot_general(
            spread, put, (((1,), (1,)), ((), ())), preferred_element_type=F32
        )
        total = term if total is None else total + term
    return total


def row_of(ref, row):
    return ref[pl.ds(row, 1), :]


def shifted_rows(a, low, high):
    count = a.shape[0]
    row = lax.broadcasted_iota(I32, a.shape, 0)
    up = jnp.where(row == count - 1, high, pltpu.roll(a, count - 1, 0))
    down = jnp.where(row == 0, low, pltpu.roll(a, 1, 0))
    return up - down


def shifted_lanes(a):
    count = a.shape[1]
    lane = lax.broadcasted_iota(I32, a.shape, 1)
    up = jnp.where(lane == count - 1, 0.0, pltpu.roll(a, count - 1, 1))
    down = jnp.where(lane == 0, 0.0, pltpu.roll(a, 1, 1))
    return up - down


def send_edges(sz, depth, plan, parts_d, parts_p, plane, refs):
    to_da, to_db, to_pa, to_pb = refs
    even_d, even_p = depth % 2 == 0, plan % 2 == 0
    cx, cz = sz.cx, sz.cz
    for i, c in enumerate(parts_d):
        first, last = plane(c, 0), plane(c, cz - 1)
        to_da[i * cx : (i + 1) * cx, :] = jnp.where(even_d, last, first)
        to_db[i * cx : (i + 1) * cx, :] = jnp.where(even_d, first, last)
    for i, c in enumerate(parts_p):
        for z in range(cz):
            a = plane(c, z)
            first, last = a[0:1], a[cx - 1 : cx]
            to_pa[i * cz + z : i * cz + z + 1, :] = jnp.where(even_p, last, first)
            to_pb[i * cz + z : i * cz + z + 1, :] = jnp.where(even_p, first, last)


def store_split(sz, source, parts, rows, refs):
    for c in range(parts):
        high, low = split(source(c))
        refs[0][c * rows : (c + 1) * rows, :] = high
        refs[1][c * rows : (c + 1) * rows, :] = low


def gather_cells(sz, table, ids, out):
    def body(j, carry):
        got = gather_chunk(table, row_of(ids, j), row_of(ids, sz.kn + j), 3, sz.rows)
        for c in range(3):
            out[pl.ds(c * sz.kn + j, 1), :] = got[c]
        return carry

    lax.fori_loop(0, sz.kn, body, 0)


def scatter_sets(sz, parts, sets, ids, acc):
    acc[...] = jnp.zeros_like(acc)

    def body(t, carry):
        s, j = t // sz.kn, lax.rem(t, sz.kn)
        one, index = sets.at[s], ids.at[s]
        values = [row_of(one, c * sz.kn + j) for c in range(parts)]
        acc[...] += scatter_chunk(values, row_of(index, j), row_of(index, sz.kn + j), sz.wp)
        return carry

    lax.fori_loop(0, sz.np * sz.kn, body, 0)


def sort_sets(sz, plan, own, got, sets, rows, offset):
    a, b, others = got
    index = [plan, lax.rem(plan + 1 - 2 * (plan % 2) + sz.np, sz.np), partner_b(plan, sz.np)]
    sets[index[1]] = a[offset : offset + rows, :]
    sets[index[2]] = b[offset : offset + rows, :]
    for shift, ref in zip(range(2, sz.np - 1), others):
        sets[lax.rem(plan + sz.np - shift, sz.np)] = ref[...]
    sets[index[0]] = own[...]


def send_sums(sz, depth, parts, acc, to_da, to_db, offset):
    even = depth % 2 == 0
    pr = sz.pr
    for c in range(parts):
        first = acc[c * sz.wp : c * sz.wp + pr, :]
        last = acc[c * sz.wp + 2 * pr : c * sz.wp + 3 * pr, :]
        to_da[offset + c * pr : offset + (c + 1) * pr, :] = jnp.where(even, last, first)
        to_db[offset + c * pr : offset + (c + 1) * pr, :] = jnp.where(even, first, last)


def own_sums(sz, parts, acc, out):
    for c in range(parts):
        out[c * sz.pr : (c + 1) * sz.pr, :] = acc[
            c * sz.wp + sz.pr : c * sz.wp + 2 * sz.pr, :
        ]


def total_sum(sz, depth, c, mine, from_da, from_db, offset):
    rows = slice(offset + c * sz.pr, offset + (c + 1) * sz.pr)
    low, high = low_high(depth, sz.nd, from_da, from_db, (rows, slice(None)))
    return low + mine[c * sz.pr : (c + 1) * sz.pr, :] + high


def moved_pile(sz, c, pile, jack, mass, count, summed):
    rows = slice(c * sz.pr, (c + 1) * sz.pr)
    p = pile[rows, :]
    return p + time_step * (jack[rows, :] - (count * p - summed)) / mass[...]


def first_kernel(
    sz, stress, velocity, pile_in, mass_in, jack_in, elem_in, cell_in,
    to_da, to_db, to_pa, to_pb, to_all, cell_ids, elem_ids, pile, mass, jack,
    high, low,
):
    depth, plan = lax.axis_index("depth"), lax.axis_index("plan")
    kn, pr = sz.kn, sz.pr
    for j in range(kn):
        lanes = slice(j * COLS, (j + 1) * COLS)
        cell, elem = cell_in[:, lanes], elem_in[:, lanes]
        cell_ids[j : j + 1, :] = lax.shift_right_arithmetic(cell, 8)
        cell_ids[kn + j : kn + j + 1, :] = lax.bitwise_and(cell, COLS - 1)
        elem_ids[j : j + 1, :] = lax.shift_right_arithmetic(elem, 8)
        elem_ids[kn + j : kn + j + 1, :] = lax.bitwise_and(elem, COLS - 1)
        to_all[3 * kn + j : 3 * kn + j + 1, :] = jnp.where(cell >= 0, 1.0, 0.0)
        to_all[4 * kn + j : 4 * kn + j + 1, :] = elem.astype(F32)
    for r in range(pr):
        lanes = slice(r * COLS, (r + 1) * COLS)
        for c in range(3):
            pile[c * pr + r : c * pr + r + 1, :] = pile_in[c : c + 1, lanes]
            jack[c * pr + r : c * pr + r + 1, :] = jack_in[c : c + 1, lanes]
        mass[r : r + 1, :] = mass_in[:, lanes]
    store_split(sz, lambda c: velocity[c], 3, sz.rows, (high, low))
    gather_cells(sz, (high, low), cell_ids, to_all)
    head = 3 * sz.cx
    to_da[head:, :] = pile[...]
    to_db[head:, :] = pile[...]
    head = 3 * sz.cz
    to_pa[head:, :] = to_all[...]
    to_pb[head:, :] = to_all[...]
    plane = lambda c, z: stress[c, z * sz.cx : (z + 1) * sz.cx, :]
    send_edges(sz, depth, plan, DEPTH_PART, PLAN_PART, plane, (to_da, to_db, to_pa, to_pb))


def velocity_update(
    sz, depth, plan, stress, velocity, density, from_da, from_db, from_pa, from_pb,
    window_of, at_cells, cell_ids, elem_ids, out, high, low, on_cells,
):
    kn, rows, wp, cx, cz = sz.kn, sz.rows, sz.wp, sz.cx, sz.cz
    pile_high, pile_low = high.at[0 : 3 * wp, :], low.at[0 : 3 * wp, :]
    pad = jnp.zeros((wp - 3 * sz.pr, COLS), F32)
    for c in range(3):
        table = jnp.concatenate(list(window_of(c)) + ([pad] if pad.shape[0] else []), axis=0)
        hi, lo = split(table)
        pile_high[c * wp : (c + 1) * wp, :] = hi
        pile_low[c * wp : (c + 1) * wp, :] = lo
    on_cells[...] = jnp.zeros_like(on_cells)

    def body(j, carry):
        at_pile = gather_chunk(
            (pile_high, pile_low), row_of(elem_ids, j), row_of(elem_ids, kn + j), 3, wp
        )
        push = [at_pile[c] - row_of(at_cells, c * kn + j) for c in range(3)]
        on_cells[...] += scatter_chunk(
            push, row_of(cell_ids, j), row_of(cell_ids, kn + j), rows
        )
        return carry

    lax.fori_loop(0, kn, body, 0)
    plane = lambda c, z: stress[c, z * cx : (z + 1) * cx, :]
    d_low, d_high = low_high(
        depth, sz.nd, from_da, from_db, (slice(0, 3 * cx), slice(None))
    )
    p_low, p_high = low_high(plan, sz.np, from_pa, from_pb, (slice(0, 3 * cz), slice(None)))
    for z in range(cz):
        here = slice(z * cx, (z + 1) * cx)
        scale = time_step / density[here, :]
        for i in range(3):
            ahead = plane(DEPTH_PART[i], z + 1) if z + 1 < cz else d_high[i * cx : (i + 1) * cx]
            behind = plane(DEPTH_PART[i], z - 1) if z > 0 else d_low[i * cx : (i + 1) * cx]
            row = slice(i * cz + z, i * cz + z + 1)
            twice = (
                (ahead - behind)
                + shifted_rows(plane(PLAN_PART[i], z), p_low[row], p_high[row])
                + shifted_lanes(plane(LAST_PART[i], z))
            )
            force = 0.5 * twice + on_cells[i * rows + z * cx : i * rows + (z + 1) * cx, :]
            out[i, here, :] = velocity[i, here, :] + scale * force


def stress_update(
    sz, depth, plan, stress, velocity, flags, from_da, from_db, from_pa, from_pb, out
):
    cx, cz = sz.cx, sz.cz
    plane = lambda c, z: velocity[c, z * cx : (z + 1) * cx, :]
    d_low, d_high = low_high(
        depth, sz.nd, from_da, from_db, (slice(0, 3 * cx), slice(None))
    )
    p_low, p_high = low_high(plan, sz.np, from_pa, from_pb, (slice(0, 3 * cz), slice(None)))
    for z in range(cz):
        here = slice(z * cx, (z + 1) * cx)
        v = [plane(c, z) for c in range(3)]
        along_z, along_x = [], []
        for c in range(3):
            ahead = plane(c, z + 1) if z + 1 < cz else d_high[c * cx : (c + 1) * cx]
            behind = plane(c, z - 1) if z > 0 else d_low[c * cx : (c + 1) * cx]
            along_z.append(ahead - behind)
            row = slice(c * cz + z, c * cz + z + 1)
            along_x.append(shifted_rows(v[c], p_low[row], p_high[row]))
        along_y = [shifted_lanes(v[c]) for c in range(3)]
        normal = [along_z[0], along_x[1], along_y[2]]
        shear = [along_x[0] + along_z[1], along_y[0] + along_z[2], along_y[1] + along_x[2]]
        bulk = (0.5 * time_step) * (normal[0] + normal[1] + normal[2])
        trial = [stress[c, here, :] + (time_step * normal[c] + bulk) for c in range(3)]
        sheared = [
            stress[3 + c, here, :] + (0.5 * time_step) * shear[c] for c in range(3)
        ]
        pressure = (trial[0] + trial[1] + trial[2]) * (1.0 / 3.0)
        dev = [t - pressure for t in trial]
        second = 0.5 * (dev[0] * dev[0] + dev[1] * dev[1] + dev[2] * dev[2])
        for t in sheared:
            second = second + t * t
        shrink = 1.0 / (1.0 + cone_rate * jnp.sqrt(second))
        flag = flags[here, :]
        factor = jnp.where(flag == 1, shrink, 0.0)
        elastic = flag == 0
        for c in range(3):
            out[c, here, :] = jnp.where(elastic, trial[c], dev[c] * factor + pressure)
            out[3 + c, here, :] = jnp.where(elastic, sheared[c], sheared[c] * factor)


def window_from(sz, depth, pile, from_da, from_db, offset):
    def of(c):
        rows = slice(offset + c * sz.pr, offset + (c + 1) * sz.pr)
        low, high = low_high(depth, sz.nd, from_da, from_db, (rows, slice(None)))
        return low, pile[c * sz.pr : (c + 1) * sz.pr, :], high

    return of


def velocity_kernel(sz, step, *refs):
    depth, plan = lax.axis_index("depth"), lax.axis_index("plan")
    refs = list(refs)
    take = lambda n: [refs.pop(0) for _ in range(n)]
    stress, velocity, density, cell_ids, elem_ids, at_cells = take(6)
    from_da, from_db, from_pa, from_pb = take(4)
    others = sz.np - 3 if sz.np > 3 else 0
    head_d, head_p, pr3 = 3 * sz.cx, 3 * sz.cz, 3 * sz.pr
    if step == 0:
        from_others = take(others)
        (pile,) = take(1)
        out, to_da, to_db, to_pa, to_pb, to_all, set_ids, mine = take(8)
        high, low, on_cells, sets, acc = take(5)
        window_of = window_from(sz, depth, pile, from_da, from_db, head_d)
    elif step == 1:
        pile, mass, jack, count, mine = take(5)
        out, to_da, to_db, to_pa, to_pb, to_all, new_pile = take(7)
        high, low, on_cells = take(3)
        window_of = window_from(sz, depth, pile, from_da, from_db, head_d)
    else:
        pile, mass, jack, count, mine, pile_da, pile_db = take(7)
        out, to_da, to_db, to_pa, to_pb, pile_out = take(6)
        high, low, on_cells, new_pile = take(4)
        window_of = window_from(sz, depth, pile, pile_da, pile_db, head_d)
    velocity_update(
        sz, depth, plan, stress, velocity, density, from_da, from_db, from_pa, from_pb,
        window_of, at_cells, cell_ids, elem_ids, out, high, low, on_cells,
    )
    if step < 2:
        store_split(sz, lambda c: out[c], 3, sz.rows, (high, low))
        gather_cells(sz, (high, low), cell_ids, to_all)
        to_pa[head_p:, :] = to_all[...]
        to_pb[head_p:, :] = to_all[...]
    if step == 0:
        kn = sz.kn
        sort_sets(sz, plan, at_cells, (from_pa, from_pb, from_others), sets, 5 * kn, head_p)
        for s in range(sz.np):
            elem = sets[s, 4 * kn : 5 * kn, :].astype(I32)
            set_ids[s, 0:kn, :] = lax.shift_right_arithmetic(elem, 8)
            set_ids[s, kn : 2 * kn, :] = lax.bitwise_and(elem, COLS - 1)
        scatter_sets(sz, 4, sets, set_ids, acc)
        send_sums(sz, depth, 4, acc, to_da, to_db, head_d)
        own_sums(sz, 4, acc, mine)
    else:
        offset = head_d + (pr3 if step == 1 else 0)
        for c in range(3):
            summed = total_sum(sz, depth, c, mine, from_da, from_db, offset)
            new_pile[c * sz.pr : (c + 1) * sz.pr, :] = moved_pile(
                sz, c, pile, jack, mass, count[...], summed
            )
        if step == 1:
            to_da[head_d:, :] = new_pile[...]
            to_db[head_d:, :] = new_pile[...]
        else:
            for r in range(sz.pr):
                for c in range(3):
                    pile_out[c : c + 1, r * COLS : (r + 1) * COLS] = new_pile[
                        c * sz.pr + r : c * sz.pr + r + 1, :
                    ]
    plane = lambda c, z: out[c, z * sz.cx : (z + 1) * sz.cx, :]
    send_edges(sz, depth, plan, (0, 1, 2), (0, 1, 2), plane, (to_da, to_db, to_pa, to_pb))


def stress_kernel(sz, step, *refs):
    depth, plan = lax.axis_index("depth"), lax.axis_index("plan")
    refs = list(refs)
    take = lambda n: [refs.pop(0) for _ in range(n)]
    stress, velocity, flags, from_da, from_db, from_pa, from_pb = take(7)
    head_d, head_p, pr3 = 3 * sz.cx, 3 * sz.cz, 3 * sz.pr
    if step == STEPS - 1:
        (out,) = take(1)
        stress_update(
            sz, depth, plan, stress, velocity, flags, from_da, from_db, from_pa, from_pb, out
        )
        return
    from_others = take(max(sz.np - 3, 0))
    own, set_ids = take(2)
    if step == 0:
        pile, mass, jack, mine_before = take(4)
        out, to_da, to_db, to_pa, to_pb, mine, new_pile, count = take(8)
    else:
        out, to_da, to_db, to_pa, to_pb, mine = take(6)
    sets, acc = take(2)
    stress_update(
        sz, depth, plan, stress, velocity, flags, from_da, from_db, from_pa, from_pb, out
    )
    sort_sets(sz, plan, own, (from_pa, from_pb, from_others), sets, 3 * sz.kn, head_p)
    scatter_sets(sz, 3, sets, set_ids, acc)
    own_sums(sz, 3, acc, mine)
    offset = head_d
    if step == 0:
        count[...] = total_sum(sz, depth, 3, mine_before, from_da, from_db, head_d)
        for c in range(3):
            summed = total_sum(sz, depth, c, mine_before, from_da, from_db, head_d)
            new_pile[c * sz.pr : (c + 1) * sz.pr, :] = moved_pile(
                sz, c, pile, jack, mass, count[...], summed
            )
        to_da[offset : offset + pr3, :] = new_pile[...]
        to_db[offset : offset + pr3, :] = new_pile[...]
        offset += pr3
    send_sums(sz, depth, 3, acc, to_da, to_db, offset)
    plane = lambda c, z: out[c, z * sz.cx : (z + 1) * sz.cx, :]
    send_edges(sz, depth, plan, DEPTH_PART, PLAN_PART, plane, (to_da, to_db, to_pa, to_pb))


def call(body, name, ins, outs, scratch=()):
    vmem = pl.BlockSpec(memory_space=pltpu.VMEM)
    return pl.pallas_call(
        body,
        out_shape=[jax.ShapeDtypeStruct(shape, dtype) for shape, dtype in outs],
        in_specs=[vmem] * len(ins),
        out_specs=[vmem] * len(outs),
        scratch_shapes=[pltpu.VMEM(shape, dtype) for shape, dtype in scratch],
        compiler_params=pltpu.CompilerParams(vmem_limit_bytes=48 * 2**20),
        name=name,
    )(*ins)


def matchings(count):
    first = [(i, i ^ 1) for i in range(count)]
    second = [(i, (i - 1) % count if i % 2 == 0 else (i + 1) % count) for i in range(count)]
    return first, second


def shards(
    stress, velocity, density, flags, pile_velocity, pile_mass, jack_force, pair_elem, pair_cell
):
    sz = Sizes(stress, pile_velocity, pair_cell)
    cz, cx, cy, rows, kn, pr = sz.cz, sz.cx, sz.cy, sz.rows, sz.kn, sz.pr
    assert cy == COLS and sz.pile % COLS == 0 and sz.pairs % COLS == 0
    assert sz.nd % 2 == 0 and sz.np % 2 == 0
    d_first, d_second = matchings(sz.nd)
    p_first, p_second = matchings(sz.np)

    def swap(da, db, pa, pb):
        pb = lax.ppermute(pb, "plan", p_second)
        pa = lax.ppermute(pa, "plan", p_first)
        db = lax.ppermute(db, "depth", d_second)
        da = lax.ppermute(da, "depth", d_first)
        return [da, db, pa, pb]

    def to_others(x):
        shifts = range(2, sz.np - 1)
        return [
            lax.ppermute(x, "plan", [(i, (i + s) % sz.np) for i in range(sz.np)]) for s in shifts
        ]

    full_shape = stress.shape, velocity.shape
    stress = stress.reshape(6, rows, cy)
    velocity = velocity.reshape(3, rows, cy)
    density = density.reshape(rows, cy)
    flags = flags.reshape(rows, cy)
    head_d, head_p, pr3, wp = 3 * cx, 3 * cz, 3 * pr, sz.wp
    big = max(3 * rows, 3 * wp)
    tables = [((big, COLS), BF16)] * 2
    cells = [((3 * rows, COLS), F32)]

    def edges(extra_d, extra_p):
        return [((head_d + extra_d, COLS), F32)] * 2 + [((head_p + extra_p, COLS), F32)] * 2

    to = call(
        functools.partial(first_kernel, sz),
        "first",
        [
            stress, velocity, pile_velocity, pile_mass.reshape(1, -1), jack_force, pair_elem,
            pair_cell,
        ],
        edges(pr3, 5 * kn)
        + [
            ((5 * kn, COLS), F32), ((2 * kn, COLS), I32), ((2 * kn, COLS), I32),
            ((pr3, COLS), F32), ((pr, COLS), F32), ((pr3, COLS), F32),
        ],
        tables,
    )
    at_cells, cell_ids, elem_ids, pile, mass, jack = to[4:]
    others = to_others(at_cells)
    got = swap(*to[:4])

    first = call(
        functools.partial(velocity_kernel, sz, 0),
        "velocity_0",
        [stress, velocity, density, cell_ids, elem_ids, at_cells, *got, *others, pile],
        [((3, rows, cy), F32)]
        + edges(4 * pr, 3 * kn)
        + [((3 * kn, COLS), F32), ((sz.np, 2 * kn, COLS), I32), ((4 * pr, COLS), F32)],
        tables
        + cells
        + [((sz.np, 5 * kn, COLS), F32), ((4 * wp, COLS), F32)],
    )
    velocity, (at_cells, set_ids, mine) = first[0], first[5:]
    others = to_others(at_cells)
    got = swap(*first[1:5])
    second = call(
        functools.partial(stress_kernel, sz, 0),
        "stress_0",
        [stress, velocity, flags, *got, *others, at_cells, set_ids, pile, mass, jack, mine],
        [((6, rows, cy), F32)]
        + edges(2 * pr3, 0)
        + [((pr3, COLS), F32), ((pr3, COLS), F32), ((pr, COLS), F32)],
        [((sz.np, 3 * kn, COLS), F32), ((3 * wp, COLS), F32)],
    )
    stress, (mine, pile, count) = second[0], second[5:]
    got = swap(*second[1:5])

    first = call(
        functools.partial(velocity_kernel, sz, 1),
        "velocity_1",
        [
            stress, velocity, density, cell_ids, elem_ids, at_cells, *got, pile, mass, jack,
            count, mine,
        ],
        [((3, rows, cy), F32)]
        + edges(pr3, 3 * kn)
        + [((3 * kn, COLS), F32), ((pr3, COLS), F32)],
        tables + cells,
    )
    velocity, (at_cells, pile) = first[0], first[5:]
    others = to_others(at_cells)
    got = swap(*first[1:5])
    pile_da, pile_db = got[0], got[1]
    second = call(
        functools.partial(stress_kernel, sz, 1),
        "stress_1",
        [stress, velocity, flags, *got, *others, at_cells, set_ids],
        [((6, rows, cy), F32)] + edges(pr3, 0) + [((pr3, COLS), F32)],
        [((sz.np, 3 * kn, COLS), F32), ((3 * wp, COLS), F32)],
    )
    stress, mine = second[0], second[5]
    got = swap(*second[1:5])

    first = call(
        functools.partial(velocity_kernel, sz, 2),
        "velocity_2",
        [
            stress, velocity, density, cell_ids, elem_ids, at_cells, *got, pile, mass, jack,
            count, mine, pile_da, pile_db,
        ],
        [((3, rows, cy), F32)] + edges(0, 0) + [(pile_velocity.shape, F32)],
        tables + cells + [((pr3, COLS), F32)],
    )
    velocity, pile_velocity = first[0], first[5]
    got = swap(*first[1:5])
    (stress,) = call(
        functools.partial(stress_kernel, sz, 2),
        "stress_2",
        [stress, velocity, flags, *got],
        [((6, rows, cy), F32)],
    )
    return stress.reshape(full_shape[0]), velocity.reshape(full_shape[1]), pile_velocity


def solution(mesh):
    cells, field = P("depth", "plan", None), P(None, "depth", "plan", None)
    pile, pairs = P(None, "depth"), P("depth", "plan")
    return jax.shard_map(
        shards,
        mesh=mesh,
        in_specs=(field, field, cells, cells, pile, P("depth"), pile, pairs, pairs),
        out_specs=(field, field, pile),
        check_vma=False,
    )
```

```python
import functools
import math

import jax
import jax.numpy as jnp
from jax import lax
from jax.experimental import pallas as pl
from jax.experimental.pallas import tpu as pltpu
from jax.sharding import PartitionSpec as P

STEPS = 3
time_step = 0.2
cone_rate = 1.5
F32, BF16, I32 = jnp.float32, jnp.bfloat16, jnp.int32
COLS = 256
DEPTH_PART = (0, 3, 4)
PLAN_PART = (3, 1, 5)
LAST_PART = (4, 5, 2)


class Sizes:
    def __init__(self, stress, pile_velocity, pair_cell):
        self.cz, self.cx, self.cy = stress.shape[1:]
        self.rows = self.cz * self.cx
        self.pile = pile_velocity.shape[1]
        self.pr = self.pile // COLS
        self.wp = 3 * self.pr
        self.pairs = pair_cell.shape[1]
        self.kn = self.pairs // COLS
        self.nd = lax.axis_size("depth")
        self.np = lax.axis_size("plan")


def partner_b(index, count):
    return jnp.where(
        index % 2 == 0, lax.rem(index + count - 1, count), lax.rem(index + 1, count)
    )


def low_high(index, count, ref_a, ref_b, where):
    a, b = ref_a[where], ref_b[where]
    even = index % 2 == 0
    zero = jnp.zeros_like(a)
    low = jnp.where(index > 0, jnp.where(even, b, a), zero)
    high = jnp.where(index < count - 1, jnp.where(even, a, b), zero)
    return low, high


def split(x):
    high = x.astype(BF16)
    return high, (x - high.astype(F32)).astype(BF16)


def hits(ids, count):
    return lax.broadcasted_iota(I32, (count, ids.shape[1]), 0) == ids


def one_hot(ids, count):
    return jnp.where(hits(ids, count), 1.0, 0.0).astype(BF16)


def gather_chunk(table, row_ids, col_ids, parts, rows):
    pick = one_hot(col_ids, COLS)
    got = jnp.dot(table[0][...], pick, preferred_element_type=F32)
    got = got + jnp.dot(table[1][...], pick, preferred_element_type=F32)
    mask = hits(row_ids, rows)
    return [
        jnp.sum(jnp.where(mask, got[c * rows : (c + 1) * rows], 0.0), axis=0, keepdims=True)
        for c in range(parts)
    ]


def scatter_chunk(values, row_ids, col_ids, rows):
    put = one_hot(col_ids, COLS)
    mask = hits(row_ids, rows)
    total = None
    for piece in zip(*[split(v) for v in values]):
        spread = jnp.concatenate(
            [jnp.where(mask, v.astype(F32), 0.0) for v in piece], axis=0
        ).astype(BF16)
        term = lax.dot_general(
            spread, put, (((1,), (1,)), ((), ())), preferred_element_type=F32
        )
        total = term if total is None else total + term
    return total


def row_of(ref, row):
    return ref[row : row + 1, :]


def shifted_rows(a, low, high):
    count = a.shape[0]
    row = lax.broadcasted_iota(I32, a.shape, 0)
    up = jnp.where(row == count - 1, high, pltpu.roll(a, count - 1, 0))
    down = jnp.where(row == 0, low, pltpu.roll(a, 1, 0))
    return up - down


def shifted_lanes(a):
    count = a.shape[1]
    lane = lax.broadcasted_iota(I32, a.shape, 1)
    up = jnp.where(lane == count - 1, 0.0, pltpu.roll(a, count - 1, 1))
    down = jnp.where(lane == 0, 0.0, pltpu.roll(a, 1, 1))
    return up - down


def send_edges(sz, depth, plan, parts_d, parts_p, plane, refs):
    to_da, to_db, to_pa, to_pb = refs
    even_d, even_p = depth % 2 == 0, plan % 2 == 0
    cx, cz = sz.cx, sz.cz
    for i, c in enumerate(parts_d):
        first, last = plane(c, 0), plane(c, cz - 1)
        to_da[i * cx : (i + 1) * cx, :] = jnp.where(even_d, last, first)
        to_db[i * cx : (i + 1) * cx, :] = jnp.where(even_d, first, last)
    for i, c in enumerate(parts_p):
        for z in range(cz):
            a = plane(c, z)
            first, last = a[0:1], a[cx - 1 : cx]
            to_pa[i * cz + z : i * cz + z + 1, :] = jnp.where(even_p, last, first)
            to_pb[i * cz + z : i * cz + z + 1, :] = jnp.where(even_p, first, last)


def store_split(sz, source, parts, rows, refs):
    for c in range(parts):
        high, low = split(source(c))
        refs[0][c * rows : (c + 1) * rows, :] = high
        refs[1][c * rows : (c + 1) * rows, :] = low


def gather_cells(sz, table, ids, out):
    for j in range(sz.kn):
        got = gather_chunk(table, row_of(ids, j), row_of(ids, sz.kn + j), 3, sz.rows)
        for c in range(3):
            out[c * sz.kn + j : c * sz.kn + j + 1, :] = got[c]


def scatter_sets(sz, parts, sets, ids, acc):
    group = math.gcd(sz.np, 4)
    acc[...] = jnp.zeros_like(acc)

    def body(t, carry):
        total = None
        for s in range(group):
            one, index = sets.at[t * group + s], ids.at[t * group + s]
            for j in range(sz.kn):
                values = [row_of(one, c * sz.kn + j) for c in range(parts)]
                term = scatter_chunk(
                    values, row_of(index, j), row_of(index, sz.kn + j), sz.wp
                )
                total = term if total is None else total + term
        acc[...] += total
        return carry

    if group == sz.np:
        body(0, 0)
    else:
        lax.fori_loop(0, sz.np // group, body, 0)


def sort_sets(sz, plan, own, got, sets, rows, offset):
    a, b, others = got
    index = [plan, lax.rem(plan + 1 - 2 * (plan % 2) + sz.np, sz.np), partner_b(plan, sz.np)]
    sets[index[1]] = a[offset : offset + rows, :]
    sets[index[2]] = b[offset : offset + rows, :]
    for shift, ref in zip(range(2, sz.np - 1), others):
        sets[lax.rem(plan + sz.np - shift, sz.np)] = ref[...]
    sets[index[0]] = own[...]


def send_sums(sz, depth, parts, acc, to_da, to_db, offset):
    even = depth % 2 == 0
    pr = sz.pr
    for c in range(parts):
        first = acc[c * sz.wp : c * sz.wp + pr, :]
        last = acc[c * sz.wp + 2 * pr : c * sz.wp + 3 * pr, :]
        to_da[offset + c * pr : offset + (c + 1) * pr, :] = jnp.where(even, last, first)
        to_db[offset + c * pr : offset + (c + 1) * pr, :] = jnp.where(even, first, last)


def own_sums(sz, parts, acc, out):
    for c in range(parts):
        out[c * sz.pr : (c + 1) * sz.pr, :] = acc[
            c * sz.wp + sz.pr : c * sz.wp + 2 * sz.pr, :
        ]


def total_sum(sz, depth, c, mine, from_da, from_db, offset):
    rows = slice(offset + c * sz.pr, offset + (c + 1) * sz.pr)
    low, high = low_high(depth, sz.nd, from_da, from_db, (rows, slice(None)))
    return low + mine[c * sz.pr : (c + 1) * sz.pr, :] + high


def moved_pile(sz, c, pile, jack, mass, count, summed):
    rows = slice(c * sz.pr, (c + 1) * sz.pr)
    p = pile[rows, :]
    return p + time_step * (jack[rows, :] - (count * p - summed)) / mass[...]


def first_kernel(sz, *refs):
    refs = list(refs)
    take = lambda n: [refs.pop(0) for _ in range(n)]
    sources = take(9)
    to_da, to_db, to_pa, to_pb, to_all, cell_ids, elem_ids, pile, mass, jack = take(10)
    stress, velocity, density, flags = take(4)
    high, low, pile_in, mass_in, jack_in, elem_in, cell_in, sems = take(8)
    targets = (
        cell_in, velocity, elem_in, pile_in, mass_in, jack_in, stress, density, flags,
    )
    copies = [
        pltpu.make_async_copy(a, b, sems.at[i]) for i, (a, b) in enumerate(zip(sources, targets))
    ]
    for copy in copies:
        copy.start()
    depth, plan = lax.axis_index("depth"), lax.axis_index("plan")
    kn, pr = sz.kn, sz.pr
    for copy in copies[:3]:
        copy.wait()
    for j in range(kn):
        lanes = slice(j * COLS, (j + 1) * COLS)
        cell, elem = cell_in[:, lanes], elem_in[:, lanes]
        cell_ids[j : j + 1, :] = lax.shift_right_arithmetic(cell, 8)
        cell_ids[kn + j : kn + j + 1, :] = lax.bitwise_and(cell, COLS - 1)
        elem_ids[j : j + 1, :] = lax.shift_right_arithmetic(elem, 8)
        elem_ids[kn + j : kn + j + 1, :] = lax.bitwise_and(elem, COLS - 1)
        to_all[3 * kn + j : 3 * kn + j + 1, :] = jnp.where(cell >= 0, 1.0, 0.0)
        to_all[4 * kn + j : 4 * kn + j + 1, :] = elem.astype(F32)
    store_split(sz, lambda c: velocity[c], 3, sz.rows, (high, low))
    gather_cells(sz, (high, low), cell_ids, to_all)
    for copy in copies[3:]:
        copy.wait()
    for r in range(pr):
        lanes = slice(r * COLS, (r + 1) * COLS)
        for c in range(3):
            pile[c * pr + r : c * pr + r + 1, :] = pile_in[c : c + 1, lanes]
            jack[c * pr + r : c * pr + r + 1, :] = jack_in[c : c + 1, lanes]
        mass[r : r + 1, :] = mass_in[:, lanes]
    head = 3 * sz.cx
    to_da[head:, :] = pile[...]
    to_db[head:, :] = pile[...]
    head = 3 * sz.cz
    to_pa[head:, :] = to_all[...]
    to_pb[head:, :] = to_all[...]
    plane = lambda c, z: stress[c, z * sz.cx : (z + 1) * sz.cx, :]
    send_edges(sz, depth, plan, DEPTH_PART, PLAN_PART, plane, (to_da, to_db, to_pa, to_pb))


def velocity_update(
    sz, depth, plan, stress, velocity, density, from_da, from_db, from_pa, from_pb,
    window_of, at_cells, cell_ids, elem_ids, out, high, low, on_cells,
):
    kn, rows, wp, cx, cz = sz.kn, sz.rows, sz.wp, sz.cx, sz.cz
    pile_high, pile_low = high.at[0 : 3 * wp, :], low.at[0 : 3 * wp, :]
    pad = jnp.zeros((wp - 3 * sz.pr, COLS), F32)
    for c in range(3):
        table = jnp.concatenate(list(window_of(c)) + ([pad] if pad.shape[0] else []), axis=0)
        hi, lo = split(table)
        pile_high[c * wp : (c + 1) * wp, :] = hi
        pile_low[c * wp : (c + 1) * wp, :] = lo
    total = None
    for j in range(kn):
        at_pile = gather_chunk(
            (pile_high, pile_low), row_of(elem_ids, j), row_of(elem_ids, kn + j), 3, wp
        )
        push = [at_pile[c] - row_of(at_cells, c * kn + j) for c in range(3)]
        term = scatter_chunk(push, row_of(cell_ids, j), row_of(cell_ids, kn + j), rows)
        total = term if total is None else total + term
    on_cells[...] = total
    plane = lambda c, z: stress[c, z * cx : (z + 1) * cx, :]
    d_low, d_high = low_high(
        depth, sz.nd, from_da, from_db, (slice(0, 3 * cx), slice(None))
    )
    p_low, p_high = low_high(plan, sz.np, from_pa, from_pb, (slice(0, 3 * cz), slice(None)))
    for z in range(cz):
        here = slice(z * cx, (z + 1) * cx)
        scale = time_step / density[here, :]
        for i in range(3):
            ahead = plane(DEPTH_PART[i], z + 1) if z + 1 < cz else d_high[i * cx : (i + 1) * cx]
            behind = plane(DEPTH_PART[i], z - 1) if z > 0 else d_low[i * cx : (i + 1) * cx]
            row = slice(i * cz + z, i * cz + z + 1)
            twice = (
                (ahead - behind)
                + shifted_rows(plane(PLAN_PART[i], z), p_low[row], p_high[row])
                + shifted_lanes(plane(LAST_PART[i], z))
            )
            force = 0.5 * twice + on_cells[i * rows + z * cx : i * rows + (z + 1) * cx, :]
            out[i, here, :] = velocity[i, here, :] + scale * force


def stress_update(
    sz, depth, plan, stress, velocity, flags, from_da, from_db, from_pa, from_pb, out
):
    cx, cz = sz.cx, sz.cz
    plane = lambda c, z: velocity[c, z * cx : (z + 1) * cx, :]
    d_low, d_high = low_high(
        depth, sz.nd, from_da, from_db, (slice(0, 3 * cx), slice(None))
    )
    p_low, p_high = low_high(plan, sz.np, from_pa, from_pb, (slice(0, 3 * cz), slice(None)))
    for z in range(cz):
        here = slice(z * cx, (z + 1) * cx)
        v = [plane(c, z) for c in range(3)]
        along_z, along_x = [], []
        for c in range(3):
            ahead = plane(c, z + 1) if z + 1 < cz else d_high[c * cx : (c + 1) * cx]
            behind = plane(c, z - 1) if z > 0 else d_low[c * cx : (c + 1) * cx]
            along_z.append(ahead - behind)
            row = slice(c * cz + z, c * cz + z + 1)
            along_x.append(shifted_rows(v[c], p_low[row], p_high[row]))
        along_y = [shifted_lanes(v[c]) for c in range(3)]
        normal = [along_z[0], along_x[1], along_y[2]]
        shear = [along_x[0] + along_z[1], along_y[0] + along_z[2], along_y[1] + along_x[2]]
        bulk = (0.5 * time_step) * (normal[0] + normal[1] + normal[2])
        trial = [stress[c, here, :] + (time_step * normal[c] + bulk) for c in range(3)]
        sheared = [
            stress[3 + c, here, :] + (0.5 * time_step) * shear[c] for c in range(3)
        ]
        pressure = (trial[0] + trial[1] + trial[2]) * (1.0 / 3.0)
        dev = [t - pressure for t in trial]
        second = 0.5 * (dev[0] * dev[0] + dev[1] * dev[1] + dev[2] * dev[2])
        for t in sheared:
            second = second + t * t
        shrink = 1.0 / (1.0 + cone_rate * jnp.sqrt(second))
        flag = flags[here, :]
        factor = jnp.where(flag == 1, shrink, 0.0)
        elastic = flag == 0
        for c in range(3):
            out[c, here, :] = jnp.where(elastic, trial[c], dev[c] * factor + pressure)
            out[3 + c, here, :] = jnp.where(elastic, sheared[c], sheared[c] * factor)


def window_from(sz, depth, pile, from_da, from_db, offset):
    def of(c):
        rows = slice(offset + c * sz.pr, offset + (c + 1) * sz.pr)
        low, high = low_high(depth, sz.nd, from_da, from_db, (rows, slice(None)))
        return low, pile[c * sz.pr : (c + 1) * sz.pr, :], high

    return of


def velocity_kernel(sz, step, *refs):
    depth, plan = lax.axis_index("depth"), lax.axis_index("plan")
    refs = list(refs)
    take = lambda n: [refs.pop(0) for _ in range(n)]
    stress, velocity, density, cell_ids, elem_ids, at_cells = take(6)
    from_da, from_db, from_pa, from_pb = take(4)
    others = sz.np - 3 if sz.np > 3 else 0
    head_d, head_p, pr3 = 3 * sz.cx, 3 * sz.cz, 3 * sz.pr
    if step == 0:
        from_others = take(others)
        (pile,) = take(1)
        out, to_da, to_db, to_pa, to_pb, to_all, set_ids, mine = take(8)
        high, low, on_cells, sets, acc = take(5)
        window_of = window_from(sz, depth, pile, from_da, from_db, head_d)
    elif step == 1:
        pile, mass, jack, count, mine = take(5)
        out, to_da, to_db, to_pa, to_pb, to_all, new_pile = take(7)
        high, low, on_cells = take(3)
        window_of = window_from(sz, depth, pile, from_da, from_db, head_d)
    else:
        pile, mass, jack, count, mine, pile_da, pile_db = take(7)
        out, to_da, to_db, to_pa, to_pb, pile_out = take(6)
        high, low, on_cells, new_pile = take(4)
        window_of = window_from(sz, depth, pile, pile_da, pile_db, head_d)
    velocity_update(
        sz, depth, plan, stress, velocity, density, from_da, from_db, from_pa, from_pb,
        window_of, at_cells, cell_ids, elem_ids, out, high, low, on_cells,
    )
    if step < 2:
        store_split(sz, lambda c: out[c], 3, sz.rows, (high, low))
        gather_cells(sz, (high, low), cell_ids, to_all)
        to_pa[head_p:, :] = to_all[...]
        to_pb[head_p:, :] = to_all[...]
    if step == 0:
        kn = sz.kn
        sort_sets(sz, plan, at_cells, (from_pa, from_pb, from_others), sets, 5 * kn, head_p)
        for s in range(sz.np):
            elem = sets[s, 4 * kn : 5 * kn, :].astype(I32)
            set_ids[s, 0:kn, :] = lax.shift_right_arithmetic(elem, 8)
            set_ids[s, kn : 2 * kn, :] = lax.bitwise_and(elem, COLS - 1)
        scatter_sets(sz, 4, sets, set_ids, acc)
        send_sums(sz, depth, 4, acc, to_da, to_db, head_d)
        own_sums(sz, 4, acc, mine)
    else:
        offset = head_d + (pr3 if step == 1 else 0)
        for c in range(3):
            summed = total_sum(sz, depth, c, mine, from_da, from_db, offset)
            new_pile[c * sz.pr : (c + 1) * sz.pr, :] = moved_pile(
                sz, c, pile, jack, mass, count[...], summed
            )
        if step == 1:
            to_da[head_d:, :] = new_pile[...]
            to_db[head_d:, :] = new_pile[...]
        else:
            for r in range(sz.pr):
                for c in range(3):
                    pile_out[c : c + 1, r * COLS : (r + 1) * COLS] = new_pile[
                        c * sz.pr + r : c * sz.pr + r + 1, :
                    ]
    plane = lambda c, z: out[c, z * sz.cx : (z + 1) * sz.cx, :]
    send_edges(sz, depth, plan, (0, 1, 2), (0, 1, 2), plane, (to_da, to_db, to_pa, to_pb))


def stress_kernel(sz, step, *refs):
    depth, plan = lax.axis_index("depth"), lax.axis_index("plan")
    refs = list(refs)
    take = lambda n: [refs.pop(0) for _ in range(n)]
    stress, velocity, flags, from_da, from_db, from_pa, from_pb = take(7)
    head_d, head_p, pr3 = 3 * sz.cx, 3 * sz.cz, 3 * sz.pr
    if step == STEPS - 1:
        (out,) = take(1)
        stress_update(
            sz, depth, plan, stress, velocity, flags, from_da, from_db, from_pa, from_pb, out
        )
        return
    from_others = take(max(sz.np - 3, 0))
    own, set_ids = take(2)
    if step == 0:
        pile, mass, jack, mine_before = take(4)
        out, to_da, to_db, to_pa, to_pb, mine, new_pile, count = take(8)
    else:
        out, to_da, to_db, to_pa, to_pb, mine = take(6)
    sets, acc = take(2)
    stress_update(
        sz, depth, plan, stress, velocity, flags, from_da, from_db, from_pa, from_pb, out
    )
    sort_sets(sz, plan, own, (from_pa, from_pb, from_others), sets, 3 * sz.kn, head_p)
    scatter_sets(sz, 3, sets, set_ids, acc)
    own_sums(sz, 3, acc, mine)
    offset = head_d
    if step == 0:
        count[...] = total_sum(sz, depth, 3, mine_before, from_da, from_db, head_d)
        for c in range(3):
            summed = total_sum(sz, depth, c, mine_before, from_da, from_db, head_d)
            new_pile[c * sz.pr : (c + 1) * sz.pr, :] = moved_pile(
                sz, c, pile, jack, mass, count[...], summed
            )
        to_da[offset : offset + pr3, :] = new_pile[...]
        to_db[offset : offset + pr3, :] = new_pile[...]
        offset += pr3
    send_sums(sz, depth, 3, acc, to_da, to_db, offset)
    plane = lambda c, z: out[c, z * sz.cx : (z + 1) * sz.cx, :]
    send_edges(sz, depth, plan, DEPTH_PART, PLAN_PART, plane, (to_da, to_db, to_pa, to_pb))


def call(body, name, ins, outs, scratch=(), copies=0):
    vmem = pl.BlockSpec(memory_space=pltpu.VMEM)
    sems = [pltpu.SemaphoreType.DMA((copies,))] if copies else []
    return pl.pallas_call(
        body,
        out_shape=[jax.ShapeDtypeStruct(shape, dtype) for shape, dtype in outs],
        in_specs=[pl.BlockSpec(memory_space=pl.ANY) if copies else vmem] * len(ins),
        out_specs=[vmem] * len(outs),
        scratch_shapes=[pltpu.VMEM(shape, dtype) for shape, dtype in scratch] + sems,
        compiler_params=pltpu.CompilerParams(vmem_limit_bytes=48 * 2**20),
        name=name,
    )(*ins)


def matchings(count):
    first = [(i, i ^ 1) for i in range(count)]
    second = [(i, (i - 1) % count if i % 2 == 0 else (i + 1) % count) for i in range(count)]
    return first, second


def shards(
    stress, velocity, density, flags, pile_velocity, pile_mass, jack_force, pair_elem, pair_cell
):
    sz = Sizes(stress, pile_velocity, pair_cell)
    cz, cx, cy, rows, kn, pr = sz.cz, sz.cx, sz.cy, sz.rows, sz.kn, sz.pr
    assert cy == COLS and sz.pile % COLS == 0 and sz.pairs % COLS == 0
    assert sz.nd % 2 == 0 and sz.np % 2 == 0
    d_first, d_second = matchings(sz.nd)
    p_first, p_second = matchings(sz.np)

    def swap(da, db, pa, pb):
        pb = lax.ppermute(pb, "plan", p_second)
        pa = lax.ppermute(pa, "plan", p_first)
        db = lax.ppermute(db, "depth", d_second)
        da = lax.ppermute(da, "depth", d_first)
        return [da, db, pa, pb]

    def to_others(x):
        shifts = range(2, sz.np - 1)
        return [
            lax.ppermute(x, "plan", [(i, (i + s) % sz.np) for i in range(sz.np)]) for s in shifts
        ]

    full_shape = stress.shape, velocity.shape
    stress = stress.reshape(6, rows, cy)
    velocity = velocity.reshape(3, rows, cy)
    density = density.reshape(rows, cy)
    flags = flags.reshape(rows, cy)
    head_d, head_p, pr3, wp = 3 * cx, 3 * cz, 3 * pr, sz.wp
    big = max(3 * rows, 3 * wp)
    tables = [((big, COLS), BF16)] * 2
    cells = [((3 * rows, COLS), F32)]

    def edges(extra_d, extra_p):
        return [((head_d + extra_d, COLS), F32)] * 2 + [((head_p + extra_p, COLS), F32)] * 2

    to = call(
        functools.partial(first_kernel, sz),
        "first",
        [
            pair_cell, velocity, pair_elem, pile_velocity, pile_mass.reshape(1, -1), jack_force,
            stress, density, flags,
        ],
        edges(pr3, 5 * kn)
        + [
            ((5 * kn, COLS), F32), ((2 * kn, COLS), I32), ((2 * kn, COLS), I32),
            ((pr3, COLS), F32), ((pr, COLS), F32), ((pr3, COLS), F32),
            (stress.shape, F32), (velocity.shape, F32), (density.shape, F32), (flags.shape, I32),
        ],
        tables
        + [(pile_velocity.shape, F32), ((1, sz.pile), F32), (jack_force.shape, F32)]
        + [(pair_elem.shape, I32), (pair_cell.shape, I32)],
        copies=9,
    )
    at_cells, cell_ids, elem_ids, pile, mass, jack = to[4:10]
    stress, velocity, density, flags = to[10:]
    others = to_others(at_cells)
    got = swap(*to[:4])

    first = call(
        functools.partial(velocity_kernel, sz, 0),
        "velocity_0",
        [stress, velocity, density, cell_ids, elem_ids, at_cells, *got, *others, pile],
        [((3, rows, cy), F32)]
        + edges(4 * pr, 3 * kn)
        + [((3 * kn, COLS), F32), ((sz.np, 2 * kn, COLS), I32), ((4 * pr, COLS), F32)],
        tables
        + cells
        + [((sz.np, 5 * kn, COLS), F32), ((4 * wp, COLS), F32)],
    )
    velocity, (at_cells, set_ids, mine) = first[0], first[5:]
    others = to_others(at_cells)
    got = swap(*first[1:5])
    second = call(
        functools.partial(stress_kernel, sz, 0),
        "stress_0",
        [stress, velocity, flags, *got, *others, at_cells, set_ids, pile, mass, jack, mine],
        [((6, rows, cy), F32)]
        + edges(2 * pr3, 0)
        + [((pr3, COLS), F32), ((pr3, COLS), F32), ((pr, COLS), F32)],
        [((sz.np, 3 * kn, COLS), F32), ((3 * wp, COLS), F32)],
    )
    stress, (mine, pile, count) = second[0], second[5:]
    got = swap(*second[1:5])

    first = call(
        functools.partial(velocity_kernel, sz, 1),
        "velocity_1",
        [
            stress, velocity, density, cell_ids, elem_ids, at_cells, *got, pile, mass, jack,
            count, mine,
        ],
        [((3, rows, cy), F32)]
        + edges(pr3, 3 * kn)
        + [((3 * kn, COLS), F32), ((pr3, COLS), F32)],
        tables + cells,
    )
    velocity, (at_cells, pile) = first[0], first[5:]
    others = to_others(at_cells)
    got = swap(*first[1:5])
    pile_da, pile_db = got[0], got[1]
    second = call(
        functools.partial(stress_kernel, sz, 1),
        "stress_1",
        [stress, velocity, flags, *got, *others, at_cells, set_ids],
        [((6, rows, cy), F32)] + edges(pr3, 0) + [((pr3, COLS), F32)],
        [((sz.np, 3 * kn, COLS), F32), ((3 * wp, COLS), F32)],
    )
    stress, mine = second[0], second[5]
    got = swap(*second[1:5])

    first = call(
        functools.partial(velocity_kernel, sz, 2),
        "velocity_2",
        [
            stress, velocity, density, cell_ids, elem_ids, at_cells, *got, pile, mass, jack,
            count, mine, pile_da, pile_db,
        ],
        [((3, rows, cy), F32)] + edges(0, 0) + [(pile_velocity.shape, F32)],
        tables + cells + [((pr3, COLS), F32)],
    )
    velocity, pile_velocity = first[0], first[5]
    got = swap(*first[1:5])
    (stress,) = call(
        functools.partial(stress_kernel, sz, 2),
        "stress_2",
        [stress, velocity, flags, *got],
        [((6, rows, cy), F32)],
    )
    return stress.reshape(full_shape[0]), velocity.reshape(full_shape[1]), pile_velocity


def solution(mesh):
    cells, field = P("depth", "plan", None), P(None, "depth", "plan", None)
    pile, pairs = P(None, "depth"), P("depth", "plan")
    return jax.shard_map(
        shards,
        mesh=mesh,
        in_specs=(field, field, cells, cells, pile, P("depth"), pile, pairs, pairs),
        out_specs=(field, field, pile),
        check_vma=False,
    )
```

```python
import functools
import math

import jax
import jax.numpy as jnp
from jax import lax
from jax.experimental import pallas as pl
from jax.experimental.pallas import tpu as pltpu
from jax.sharding import PartitionSpec as P

STEPS = 3
time_step = 0.2
cone_rate = 1.5
F32, BF16, I32 = jnp.float32, jnp.bfloat16, jnp.int32
COLS = 256
DEPTH_PART = (0, 3, 4)
PLAN_PART = (3, 1, 5)
LAST_PART = (4, 5, 2)


class Sizes:
    def __init__(self, stress, pile_velocity, pair_cell):
        self.cz, self.cx, self.cy = stress.shape[1:]
        self.rows = self.cz * self.cx
        self.pile = pile_velocity.shape[1]
        self.pr = self.pile // COLS
        self.wp = 3 * self.pr
        self.pairs = pair_cell.shape[1]
        self.kn = self.pairs // COLS
        self.nd = lax.axis_size("depth")
        self.np = lax.axis_size("plan")


def partner_b(index, count):
    return jnp.where(
        index % 2 == 0, lax.rem(index + count - 1, count), lax.rem(index + 1, count)
    )


def low_high(index, count, ref_a, ref_b, where):
    a, b = ref_a[where], ref_b[where]
    even = index % 2 == 0
    zero = jnp.zeros_like(a)
    low = jnp.where(index > 0, jnp.where(even, b, a), zero)
    high = jnp.where(index < count - 1, jnp.where(even, a, b), zero)
    return low, high


def split(x):
    high = x.astype(BF16)
    return high, (x - high.astype(F32)).astype(BF16)


def hits(ids, count):
    return lax.broadcasted_iota(I32, (count, ids.shape[1]), 0) == ids


def one_hot(ids, count):
    return jnp.where(hits(ids, count), 1.0, 0.0).astype(BF16)


def gather_chunk(table, row_ids, col_ids, parts, rows):
    pick = one_hot(col_ids, COLS)
    got = jnp.dot(table[0][...], pick, preferred_element_type=F32)
    got = got + jnp.dot(table[1][...], pick, preferred_element_type=F32)
    mask = hits(row_ids, rows)
    return [
        jnp.sum(jnp.where(mask, got[c * rows : (c + 1) * rows], 0.0), axis=0, keepdims=True)
        for c in range(parts)
    ]


def scatter_chunk(values, row_ids, col_ids, rows):
    put = one_hot(col_ids, COLS)
    mask = hits(row_ids, rows)
    total = None
    for piece in zip(*[split(v) for v in values]):
        spread = jnp.concatenate(
            [jnp.where(mask, v.astype(F32), 0.0) for v in piece], axis=0
        ).astype(BF16)
        term = lax.dot_general(
            spread, put, (((1,), (1,)), ((), ())), preferred_element_type=F32
        )
        total = term if total is None else total + term
    return total


def row_of(ref, row):
    return ref[row : row + 1, :]


def shifted_rows(a, low, high):
    count = a.shape[0]
    row = lax.broadcasted_iota(I32, a.shape, 0)
    up = jnp.where(row == count - 1, high, pltpu.roll(a, count - 1, 0))
    down = jnp.where(row == 0, low, pltpu.roll(a, 1, 0))
    return up - down


def shifted_lanes(a):
    count = a.shape[1]
    lane = lax.broadcasted_iota(I32, a.shape, 1)
    up = jnp.where(lane == count - 1, 0.0, pltpu.roll(a, count - 1, 1))
    down = jnp.where(lane == 0, 0.0, pltpu.roll(a, 1, 1))
    return up - down


def send_edges(sz, depth, plan, parts_d, parts_p, plane, refs):
    to_da, to_db, to_pa, to_pb = refs
    even_d, even_p = depth % 2 == 0, plan % 2 == 0
    cx, cz = sz.cx, sz.cz
    for i, c in enumerate(parts_d):
        first, last = plane(c, 0), plane(c, cz - 1)
        to_da[i * cx : (i + 1) * cx, :] = jnp.where(even_d, last, first)
        to_db[i * cx : (i + 1) * cx, :] = jnp.where(even_d, first, last)
    for i, c in enumerate(parts_p):
        for z in range(cz):
            a = plane(c, z)
            first, last = a[0:1], a[cx - 1 : cx]
            to_pa[i * cz + z : i * cz + z + 1, :] = jnp.where(even_p, last, first)
            to_pb[i * cz + z : i * cz + z + 1, :] = jnp.where(even_p, first, last)


def store_split(sz, source, parts, rows, refs):
    for c in range(parts):
        high, low = split(source(c))
        refs[0][c * rows : (c + 1) * rows, :] = high
        refs[1][c * rows : (c + 1) * rows, :] = low


def gather_cells(sz, table, ids, out):
    for j in range(sz.kn):
        got = gather_chunk(table, row_of(ids, j), row_of(ids, sz.kn + j), 3, sz.rows)
        for c in range(3):
            out[c * sz.kn + j : c * sz.kn + j + 1, :] = got[c]


def scatter_sets(sz, parts, sets, ids, acc):
    group = math.gcd(sz.np, 4)
    acc[...] = jnp.zeros_like(acc)

    def body(t, carry):
        total = None
        for s in range(group):
            one, index = sets.at[t * group + s], ids.at[t * group + s]
            for j in range(sz.kn):
                values = [row_of(one, c * sz.kn + j) for c in range(parts)]
                term = scatter_chunk(
                    values, row_of(index, j), row_of(index, sz.kn + j), sz.wp
                )
                total = term if total is None else total + term
        acc[...] += total
        return carry

    if group == sz.np:
        body(0, 0)
    else:
        lax.fori_loop(0, sz.np // group, body, 0)


def sort_sets(sz, plan, own, got, sets, rows, offset):
    a, b, others = got
    index = [plan, lax.rem(plan + 1 - 2 * (plan % 2) + sz.np, sz.np), partner_b(plan, sz.np)]
    sets[index[1]] = a[offset : offset + rows, :]
    sets[index[2]] = b[offset : offset + rows, :]
    for shift, ref in zip(range(2, sz.np - 1), others):
        sets[lax.rem(plan + sz.np - shift, sz.np)] = ref[...]
    sets[index[0]] = own[...]


def send_sums(sz, depth, parts, acc, to_da, to_db, offset):
    even = depth % 2 == 0
    pr = sz.pr
    for c in range(parts):
        first = acc[c * sz.wp : c * sz.wp + pr, :]
        last = acc[c * sz.wp + 2 * pr : c * sz.wp + 3 * pr, :]
        to_da[offset + c * pr : offset + (c + 1) * pr, :] = jnp.where(even, last, first)
        to_db[offset + c * pr : offset + (c + 1) * pr, :] = jnp.where(even, first, last)


def own_sums(sz, parts, acc, out):
    for c in range(parts):
        out[c * sz.pr : (c + 1) * sz.pr, :] = acc[
            c * sz.wp + sz.pr : c * sz.wp + 2 * sz.pr, :
        ]


def total_sum(sz, depth, c, mine, from_da, from_db, offset):
    rows = slice(offset + c * sz.pr, offset + (c + 1) * sz.pr)
    low, high = low_high(depth, sz.nd, from_da, from_db, (rows, slice(None)))
    return low + mine[c * sz.pr : (c + 1) * sz.pr, :] + high


def moved_pile(sz, c, pile, jack, mass, count, summed):
    rows = slice(c * sz.pr, (c + 1) * sz.pr)
    p = pile[rows, :]
    return p + time_step * (jack[rows, :] - (count * p - summed)) / mass[...]


def first_kernel(sz, *refs):
    refs = list(refs)
    take = lambda n: [refs.pop(0) for _ in range(n)]
    sources = take(9)
    to_da, to_db, to_pa, to_pb, to_all, cell_ids, elem_ids, pile, mass, jack = take(10)
    stress, velocity, density, flags = take(4)
    high, low, pile_in, mass_in, jack_in, elem_in, cell_in, sems = take(8)
    targets = (
        cell_in, velocity, elem_in, pile_in, mass_in, jack_in, stress, density, flags,
    )
    copies = [
        pltpu.make_async_copy(a, b, sems.at[i]) for i, (a, b) in enumerate(zip(sources, targets))
    ]
    for copy in copies:
        copy.start()
    depth, plan = lax.axis_index("depth"), lax.axis_index("plan")
    kn, pr = sz.kn, sz.pr
    for copy in copies[:3]:
        copy.wait()
    for j in range(kn):
        lanes = slice(j * COLS, (j + 1) * COLS)
        cell, elem = cell_in[:, lanes], elem_in[:, lanes]
        cell_ids[j : j + 1, :] = lax.shift_right_arithmetic(cell, 8)
        cell_ids[kn + j : kn + j + 1, :] = lax.bitwise_and(cell, COLS - 1)
        elem_ids[j : j + 1, :] = lax.shift_right_arithmetic(elem, 8)
        elem_ids[kn + j : kn + j + 1, :] = lax.bitwise_and(elem, COLS - 1)
        to_all[3 * kn + j : 3 * kn + j + 1, :] = jnp.where(cell >= 0, 1.0, 0.0)
        to_all[4 * kn + j : 4 * kn + j + 1, :] = elem.astype(F32)
    store_split(sz, lambda c: velocity[c], 3, sz.rows, (high, low))
    gather_cells(sz, (high, low), cell_ids, to_all)
    for copy in copies[3:]:
        copy.wait()
    for r in range(pr):
        lanes = slice(r * COLS, (r + 1) * COLS)
        for c in range(3):
            pile[c * pr + r : c * pr + r + 1, :] = pile_in[c : c + 1, lanes]
            jack[c * pr + r : c * pr + r + 1, :] = jack_in[c : c + 1, lanes]
        mass[r : r + 1, :] = mass_in[:, lanes]
    head = 3 * sz.cx
    to_da[head:, :] = pile[...]
    to_db[head:, :] = pile[...]
    head = 3 * sz.cz
    to_pa[head:, :] = to_all[...]
    to_pb[head:, :] = to_all[...]
    plane = lambda c, z: stress[c, z * sz.cx : (z + 1) * sz.cx, :]
    send_edges(sz, depth, plan, DEPTH_PART, PLAN_PART, plane, (to_da, to_db, to_pa, to_pb))


def velocity_update(
    sz, depth, plan, stress, velocity, density, from_da, from_db, from_pa, from_pb,
    window_of, at_cells, cell_ids, elem_ids, out, high, low, on_cells,
):
    kn, rows, wp, cx, cz = sz.kn, sz.rows, sz.wp, sz.cx, sz.cz
    pile_high, pile_low = high.at[0 : 3 * wp, :], low.at[0 : 3 * wp, :]
    pad = jnp.zeros((wp - 3 * sz.pr, COLS), F32)
    for c in range(3):
        table = jnp.concatenate(list(window_of(c)) + ([pad] if pad.shape[0] else []), axis=0)
        hi, lo = split(table)
        pile_high[c * wp : (c + 1) * wp, :] = hi
        pile_low[c * wp : (c + 1) * wp, :] = lo
    total = None
    for j in range(kn):
        at_pile = gather_chunk(
            (pile_high, pile_low), row_of(elem_ids, j), row_of(elem_ids, kn + j), 3, wp
        )
        push = [at_pile[c] - row_of(at_cells, c * kn + j) for c in range(3)]
        term = scatter_chunk(push, row_of(cell_ids, j), row_of(cell_ids, kn + j), rows)
        total = term if total is None else total + term
    on_cells[...] = total
    plane = lambda c, z: stress[c, z * cx : (z + 1) * cx, :]
    d_low, d_high = low_high(
        depth, sz.nd, from_da, from_db, (slice(0, 3 * cx), slice(None))
    )
    p_low, p_high = low_high(plan, sz.np, from_pa, from_pb, (slice(0, 3 * cz), slice(None)))
    for z in range(cz):
        here = slice(z * cx, (z + 1) * cx)
        scale = time_step / density[here, :]
        for i in range(3):
            ahead = plane(DEPTH_PART[i], z + 1) if z + 1 < cz else d_high[i * cx : (i + 1) * cx]
            behind = plane(DEPTH_PART[i], z - 1) if z > 0 else d_low[i * cx : (i + 1) * cx]
            row = slice(i * cz + z, i * cz + z + 1)
            twice = (
                (ahead - behind)
                + shifted_rows(plane(PLAN_PART[i], z), p_low[row], p_high[row])
                + shifted_lanes(plane(LAST_PART[i], z))
            )
            force = 0.5 * twice + on_cells[i * rows + z * cx : i * rows + (z + 1) * cx, :]
            out[i, here, :] = velocity[i, here, :] + scale * force


def stress_update(
    sz, depth, plan, stress, velocity, flags, from_da, from_db, from_pa, from_pb, out,
    plane_done=None,
):
    cx, cz = sz.cx, sz.cz
    plane = lambda c, z: velocity[c, z * cx : (z + 1) * cx, :]
    d_low, d_high = low_high(
        depth, sz.nd, from_da, from_db, (slice(0, 3 * cx), slice(None))
    )
    p_low, p_high = low_high(plan, sz.np, from_pa, from_pb, (slice(0, 3 * cz), slice(None)))
    for z in range(cz):
        here = slice(z * cx, (z + 1) * cx)
        v = [plane(c, z) for c in range(3)]
        along_z, along_x = [], []
        for c in range(3):
            ahead = plane(c, z + 1) if z + 1 < cz else d_high[c * cx : (c + 1) * cx]
            behind = plane(c, z - 1) if z > 0 else d_low[c * cx : (c + 1) * cx]
            along_z.append(ahead - behind)
            row = slice(c * cz + z, c * cz + z + 1)
            along_x.append(shifted_rows(v[c], p_low[row], p_high[row]))
        along_y = [shifted_lanes(v[c]) for c in range(3)]
        normal = [along_z[0], along_x[1], along_y[2]]
        shear = [along_x[0] + along_z[1], along_y[0] + along_z[2], along_y[1] + along_x[2]]
        bulk = (0.5 * time_step) * (normal[0] + normal[1] + normal[2])
        trial = [stress[c, here, :] + (time_step * normal[c] + bulk) for c in range(3)]
        sheared = [
            stress[3 + c, here, :] + (0.5 * time_step) * shear[c] for c in range(3)
        ]
        pressure = (trial[0] + trial[1] + trial[2]) * (1.0 / 3.0)
        dev = [t - pressure for t in trial]
        second = 0.5 * (dev[0] * dev[0] + dev[1] * dev[1] + dev[2] * dev[2])
        for t in sheared:
            second = second + t * t
        shrink = 1.0 / (1.0 + cone_rate * jnp.sqrt(second))
        flag = flags[here, :]
        factor = jnp.where(flag == 1, shrink, 0.0)
        elastic = flag == 0
        for c in range(3):
            out[c, here, :] = jnp.where(elastic, trial[c], dev[c] * factor + pressure)
            out[3 + c, here, :] = jnp.where(elastic, sheared[c], sheared[c] * factor)
        if plane_done is not None:
            plane_done(z)


def window_from(sz, depth, pile, from_da, from_db, offset):
    def of(c):
        rows = slice(offset + c * sz.pr, offset + (c + 1) * sz.pr)
        low, high = low_high(depth, sz.nd, from_da, from_db, (rows, slice(None)))
        return low, pile[c * sz.pr : (c + 1) * sz.pr, :], high

    return of


def velocity_kernel(sz, step, *refs):
    depth, plan = lax.axis_index("depth"), lax.axis_index("plan")
    refs = list(refs)
    take = lambda n: [refs.pop(0) for _ in range(n)]
    stress, velocity, density, cell_ids, elem_ids, at_cells = take(6)
    from_da, from_db, from_pa, from_pb = take(4)
    others = sz.np - 3 if sz.np > 3 else 0
    head_d, head_p, pr3 = 3 * sz.cx, 3 * sz.cz, 3 * sz.pr
    if step == 0:
        from_others = take(others)
        (pile,) = take(1)
        out, to_da, to_db, to_pa, to_pb, to_all, set_ids, mine = take(8)
        high, low, on_cells, sets, acc = take(5)
        window_of = window_from(sz, depth, pile, from_da, from_db, head_d)
    elif step == 1:
        pile, mass, jack, count, mine = take(5)
        out, to_da, to_db, to_pa, to_pb, to_all, new_pile = take(7)
        high, low, on_cells = take(3)
        window_of = window_from(sz, depth, pile, from_da, from_db, head_d)
    else:
        pile, mass, jack, count, mine, pile_da, pile_db = take(7)
        out, to_da, to_db, to_pa, to_pb, pile_out = take(6)
        high, low, on_cells, new_pile = take(4)
        window_of = window_from(sz, depth, pile, pile_da, pile_db, head_d)
    velocity_update(
        sz, depth, plan, stress, velocity, density, from_da, from_db, from_pa, from_pb,
        window_of, at_cells, cell_ids, elem_ids, out, high, low, on_cells,
    )
    if step < 2:
        store_split(sz, lambda c: out[c], 3, sz.rows, (high, low))
        gather_cells(sz, (high, low), cell_ids, to_all)
        to_pa[head_p:, :] = to_all[...]
        to_pb[head_p:, :] = to_all[...]
    if step == 0:
        kn = sz.kn
        sort_sets(sz, plan, at_cells, (from_pa, from_pb, from_others), sets, 5 * kn, head_p)
        for s in range(sz.np):
            elem = sets[s, 4 * kn : 5 * kn, :].astype(I32)
            set_ids[s, 0:kn, :] = lax.shift_right_arithmetic(elem, 8)
            set_ids[s, kn : 2 * kn, :] = lax.bitwise_and(elem, COLS - 1)
        scatter_sets(sz, 4, sets, set_ids, acc)
        send_sums(sz, depth, 4, acc, to_da, to_db, head_d)
        own_sums(sz, 4, acc, mine)
    else:
        offset = head_d + (pr3 if step == 1 else 0)
        for c in range(3):
            summed = total_sum(sz, depth, c, mine, from_da, from_db, offset)
            new_pile[c * sz.pr : (c + 1) * sz.pr, :] = moved_pile(
                sz, c, pile, jack, mass, count[...], summed
            )
        if step == 1:
            to_da[head_d:, :] = new_pile[...]
            to_db[head_d:, :] = new_pile[...]
        else:
            for r in range(sz.pr):
                for c in range(3):
                    pile_out[c : c + 1, r * COLS : (r + 1) * COLS] = new_pile[
                        c * sz.pr + r : c * sz.pr + r + 1, :
                    ]
    plane = lambda c, z: out[c, z * sz.cx : (z + 1) * sz.cx, :]
    send_edges(sz, depth, plan, (0, 1, 2), (0, 1, 2), plane, (to_da, to_db, to_pa, to_pb))


def stress_kernel(sz, step, *refs):
    depth, plan = lax.axis_index("depth"), lax.axis_index("plan")
    refs = list(refs)
    take = lambda n: [refs.pop(0) for _ in range(n)]
    stress, velocity, flags, from_da, from_db, from_pa, from_pb = take(7)
    head_d, head_p, pr3 = 3 * sz.cx, 3 * sz.cz, 3 * sz.pr
    if step == STEPS - 1:
        pile, stress_out, velocity_out, pile_out, out, sems = take(6)
        copies = [
            pltpu.make_async_copy(velocity, velocity_out, sems.at[sz.cz]),
            pltpu.make_async_copy(pile, pile_out, sems.at[sz.cz + 1]),
        ]
        for copy in copies:
            copy.start()

        def plane_done(z):
            part = (slice(None), pl.ds(z * sz.cx, sz.cx), slice(None))
            copies.append(
                pltpu.make_async_copy(out.at[part], stress_out.at[part], sems.at[z])
            )
            copies[-1].start()

        stress_update(
            sz, depth, plan, stress, velocity, flags, from_da, from_db, from_pa, from_pb, out,
            plane_done,
        )
        for copy in copies:
            copy.wait()
        return
    from_others = take(max(sz.np - 3, 0))
    own, set_ids = take(2)
    if step == 0:
        pile, mass, jack, mine_before = take(4)
        out, to_da, to_db, to_pa, to_pb, mine, new_pile, count = take(8)
    else:
        out, to_da, to_db, to_pa, to_pb, mine = take(6)
    sets, acc = take(2)
    stress_update(
        sz, depth, plan, stress, velocity, flags, from_da, from_db, from_pa, from_pb, out
    )
    sort_sets(sz, plan, own, (from_pa, from_pb, from_others), sets, 3 * sz.kn, head_p)
    scatter_sets(sz, 3, sets, set_ids, acc)
    own_sums(sz, 3, acc, mine)
    offset = head_d
    if step == 0:
        count[...] = total_sum(sz, depth, 3, mine_before, from_da, from_db, head_d)
        for c in range(3):
            summed = total_sum(sz, depth, c, mine_before, from_da, from_db, head_d)
            new_pile[c * sz.pr : (c + 1) * sz.pr, :] = moved_pile(
                sz, c, pile, jack, mass, count[...], summed
            )
        to_da[offset : offset + pr3, :] = new_pile[...]
        to_db[offset : offset + pr3, :] = new_pile[...]
        offset += pr3
    send_sums(sz, depth, 3, acc, to_da, to_db, offset)
    plane = lambda c, z: out[c, z * sz.cx : (z + 1) * sz.cx, :]
    send_edges(sz, depth, plan, DEPTH_PART, PLAN_PART, plane, (to_da, to_db, to_pa, to_pb))


def call(body, name, ins, outs, scratch=(), copies=0, far_ins=False, far_outs=False):
    vmem, far = pl.BlockSpec(memory_space=pltpu.VMEM), pl.BlockSpec(memory_space=pl.ANY)
    sems = [pltpu.SemaphoreType.DMA((copies,))] if copies else []
    return pl.pallas_call(
        body,
        out_shape=[jax.ShapeDtypeStruct(shape, dtype) for shape, dtype in outs],
        in_specs=[far if far_ins else vmem] * len(ins),
        out_specs=[far if far_outs else vmem] * len(outs),
        scratch_shapes=[pltpu.VMEM(shape, dtype) for shape, dtype in scratch] + sems,
        compiler_params=pltpu.CompilerParams(vmem_limit_bytes=48 * 2**20),
        name=name,
    )(*[pltpu.with_memory_space_constraint(x, pltpu.HBM) if far_ins else x for x in ins])


def matchings(count):
    first = [(i, i ^ 1) for i in range(count)]
    second = [(i, (i - 1) % count if i % 2 == 0 else (i + 1) % count) for i in range(count)]
    return first, second


def shards(
    stress, velocity, density, flags, pile_velocity, pile_mass, jack_force, pair_elem, pair_cell
):
    sz = Sizes(stress, pile_velocity, pair_cell)
    cz, cx, cy, rows, kn, pr = sz.cz, sz.cx, sz.cy, sz.rows, sz.kn, sz.pr
    assert cy == COLS and sz.pile % COLS == 0 and sz.pairs % COLS == 0
    assert sz.nd % 2 == 0 and sz.np % 2 == 0
    d_first, d_second = matchings(sz.nd)
    p_first, p_second = matchings(sz.np)

    def swap(da, db, pa, pb):
        pb = lax.ppermute(pb, "plan", p_second)
        pa = lax.ppermute(pa, "plan", p_first)
        db = lax.ppermute(db, "depth", d_second)
        da = lax.ppermute(da, "depth", d_first)
        return [da, db, pa, pb]

    def to_others(x):
        shifts = range(2, sz.np - 1)
        return [
            lax.ppermute(x, "plan", [(i, (i + s) % sz.np) for i in range(sz.np)]) for s in shifts
        ]

    full_shape = stress.shape, velocity.shape
    stress = stress.reshape(6, rows, cy)
    velocity = velocity.reshape(3, rows, cy)
    density = density.reshape(rows, cy)
    flags = flags.reshape(rows, cy)
    head_d, head_p, pr3, wp = 3 * cx, 3 * cz, 3 * pr, sz.wp
    big = max(3 * rows, 3 * wp)
    tables = [((big, COLS), BF16)] * 2
    cells = [((3 * rows, COLS), F32)]

    def edges(extra_d, extra_p):
        return [((head_d + extra_d, COLS), F32)] * 2 + [((head_p + extra_p, COLS), F32)] * 2

    to = call(
        functools.partial(first_kernel, sz),
        "first",
        [
            pair_cell, velocity, pair_elem, pile_velocity, pile_mass.reshape(1, -1), jack_force,
            stress, density, flags,
        ],
        edges(pr3, 5 * kn)
        + [
            ((5 * kn, COLS), F32), ((2 * kn, COLS), I32), ((2 * kn, COLS), I32),
            ((pr3, COLS), F32), ((pr, COLS), F32), ((pr3, COLS), F32),
            (stress.shape, F32), (velocity.shape, F32), (density.shape, F32), (flags.shape, I32),
        ],
        tables
        + [(pile_velocity.shape, F32), ((1, sz.pile), F32), (jack_force.shape, F32)]
        + [(pair_elem.shape, I32), (pair_cell.shape, I32)],
        copies=9,
        far_ins=True,
    )
    at_cells, cell_ids, elem_ids, pile, mass, jack = to[4:10]
    stress, velocity, density, flags = to[10:]
    others = to_others(at_cells)
    got = swap(*to[:4])

    first = call(
        functools.partial(velocity_kernel, sz, 0),
        "velocity_0",
        [stress, velocity, density, cell_ids, elem_ids, at_cells, *got, *others, pile],
        [((3, rows, cy), F32)]
        + edges(4 * pr, 3 * kn)
        + [((3 * kn, COLS), F32), ((sz.np, 2 * kn, COLS), I32), ((4 * pr, COLS), F32)],
        tables
        + cells
        + [((sz.np, 5 * kn, COLS), F32), ((4 * wp, COLS), F32)],
    )
    velocity, (at_cells, set_ids, mine) = first[0], first[5:]
    others = to_others(at_cells)
    got = swap(*first[1:5])
    second = call(
        functools.partial(stress_kernel, sz, 0),
        "stress_0",
        [stress, velocity, flags, *got, *others, at_cells, set_ids, pile, mass, jack, mine],
        [((6, rows, cy), F32)]
        + edges(2 * pr3, 0)
        + [((pr3, COLS), F32), ((pr3, COLS), F32), ((pr, COLS), F32)],
        [((sz.np, 3 * kn, COLS), F32), ((3 * wp, COLS), F32)],
    )
    stress, (mine, pile, count) = second[0], second[5:]
    got = swap(*second[1:5])

    first = call(
        functools.partial(velocity_kernel, sz, 1),
        "velocity_1",
        [
            stress, velocity, density, cell_ids, elem_ids, at_cells, *got, pile, mass, jack,
            count, mine,
        ],
        [((3, rows, cy), F32)]
        + edges(pr3, 3 * kn)
        + [((3 * kn, COLS), F32), ((pr3, COLS), F32)],
        tables + cells,
    )
    velocity, (at_cells, pile) = first[0], first[5:]
    others = to_others(at_cells)
    got = swap(*first[1:5])
    pile_da, pile_db = got[0], got[1]
    second = call(
        functools.partial(stress_kernel, sz, 1),
        "stress_1",
        [stress, velocity, flags, *got, *others, at_cells, set_ids],
        [((6, rows, cy), F32)] + edges(pr3, 0) + [((pr3, COLS), F32)],
        [((sz.np, 3 * kn, COLS), F32), ((3 * wp, COLS), F32)],
    )
    stress, mine = second[0], second[5]
    got = swap(*second[1:5])

    first = call(
        functools.partial(velocity_kernel, sz, 2),
        "velocity_2",
        [
            stress, velocity, density, cell_ids, elem_ids, at_cells, *got, pile, mass, jack,
            count, mine, pile_da, pile_db,
        ],
        [((3, rows, cy), F32)] + edges(0, 0) + [(pile_velocity.shape, F32)],
        tables + cells + [((pr3, COLS), F32)],
    )
    velocity, pile_out = first[0], first[5]
    got = swap(*first[1:5])
    stress, velocity, pile_velocity = call(
        functools.partial(stress_kernel, sz, 2),
        "stress_2",
        [stress, velocity, flags, *got, pile_out],
        [(stress.shape, F32), (velocity.shape, F32), (pile_velocity.shape, F32)],
        [(stress.shape, F32)],
        copies=cz + 2,
        far_outs=True,
    )
    return stress.reshape(full_shape[0]), velocity.reshape(full_shape[1]), pile_velocity


def solution(mesh):
    cells, field = P("depth", "plan", None), P(None, "depth", "plan", None)
    pile, pairs = P(None, "depth"), P("depth", "plan")
    return jax.shard_map(
        shards,
        mesh=mesh,
        in_specs=(field, field, cells, cells, pile, P("depth"), pile, pairs, pairs),
        out_specs=(field, field, pile),
        check_vma=False,
    )
```

```python
import functools
import math

import jax
import jax.numpy as jnp
from jax import lax
from jax.experimental import pallas as pl
from jax.experimental.pallas import tpu as pltpu
from jax.sharding import PartitionSpec as P

STEPS = 3
time_step = 0.2
cone_rate = 1.5
F32, BF16, I32 = jnp.float32, jnp.bfloat16, jnp.int32
COLS = 256
DEPTH_PART = (0, 3, 4)
PLAN_PART = (3, 1, 5)
LAST_PART = (4, 5, 2)


class Sizes:
    def __init__(self, stress, pile_velocity, pair_cell):
        self.cz, self.cx, self.cy = stress.shape[1:]
        self.rows = self.cz * self.cx
        self.pile = pile_velocity.shape[1]
        self.pr = self.pile // COLS
        self.wp = 3 * self.pr
        self.pairs = pair_cell.shape[1]
        self.kn = self.pairs // COLS
        self.nd = lax.axis_size("depth")
        self.np = lax.axis_size("plan")


def partner_b(index, count):
    return jnp.where(
        index % 2 == 0, lax.rem(index + count - 1, count), lax.rem(index + 1, count)
    )


def low_high(index, count, ref_a, ref_b, where):
    a, b = ref_a[where], ref_b[where]
    even = index % 2 == 0
    zero = jnp.zeros_like(a)
    low = jnp.where(index > 0, jnp.where(even, b, a), zero)
    high = jnp.where(index < count - 1, jnp.where(even, a, b), zero)
    return low, high


def split(x):
    high = x.astype(BF16)
    return high, (x - high.astype(F32)).astype(BF16)


def hits(ids, count):
    return lax.broadcasted_iota(I32, (count, ids.shape[1]), 0) == ids


def one_hot(ids, count):
    return jnp.where(hits(ids, count), 1.0, 0.0).astype(BF16)


def gather_chunk(table, row_ids, col_ids, parts, rows):
    pick = one_hot(col_ids, COLS)
    got = jnp.dot(table[0][...], pick, preferred_element_type=F32)
    got = got + jnp.dot(table[1][...], pick, preferred_element_type=F32)
    mask = hits(row_ids, rows)
    return [
        jnp.sum(jnp.where(mask, got[c * rows : (c + 1) * rows], 0.0), axis=0, keepdims=True)
        for c in range(parts)
    ]


def scatter_chunk(values, row_ids, col_ids, rows, exact=0):
    put = one_hot(col_ids, COLS)
    mask = hits(row_ids, rows)
    pairs = [split(v) for v in values]
    pieces = [v[0] for v in pairs], [v[1] for v in pairs[: len(values) - exact]]
    terms = []
    for piece in pieces:
        spread = jnp.concatenate(
            [jnp.where(mask, v.astype(F32), 0.0) for v in piece], axis=0
        ).astype(BF16)
        terms.append(
            lax.dot_general(spread, put, (((1,), (1,)), ((), ())), preferred_element_type=F32)
        )
    return terms


def added(total, terms):
    return terms if total is None else [a + b for a, b in zip(total, terms)]


def row_of(ref, row):
    return ref[row : row + 1, :]


def shifted_rows(a, low, high):
    count = a.shape[0]
    row = lax.broadcasted_iota(I32, a.shape, 0)
    up = jnp.where(row == count - 1, high, pltpu.roll(a, count - 1, 0))
    down = jnp.where(row == 0, low, pltpu.roll(a, 1, 0))
    return up - down


def shifted_lanes(a):
    count = a.shape[1]
    lane = lax.broadcasted_iota(I32, a.shape, 1)
    up = jnp.where(lane == count - 1, 0.0, pltpu.roll(a, count - 1, 1))
    down = jnp.where(lane == 0, 0.0, pltpu.roll(a, 1, 1))
    return up - down


def send_layers(sz, depth, parts, plane, to_da, to_db):
    even, cx = depth % 2 == 0, sz.cx
    for i, c in enumerate(parts):
        first, last = plane(c, 0), plane(c, sz.cz - 1)
        to_da[i * cx : (i + 1) * cx, :] = jnp.where(even, last, first)
        to_db[i * cx : (i + 1) * cx, :] = jnp.where(even, first, last)


def column(sz, ref, c, x):
    rows = [z * sz.cx + x for z in range(sz.cz)]
    return jnp.concatenate([ref[c, r : r + 1, :] for r in rows], axis=0)


def send_columns(sz, plan, columns, to_pa, to_pb):
    even, cz = plan % 2 == 0, sz.cz
    for i, (first, last) in enumerate(columns):
        to_pa[i * cz : (i + 1) * cz, :] = jnp.where(even, last, first)
        to_pb[i * cz : (i + 1) * cz, :] = jnp.where(even, first, last)


def store_split(sz, source, parts, rows, refs):
    for c in range(parts):
        high, low = split(source(c))
        refs[0][c * rows : (c + 1) * rows, :] = high
        refs[1][c * rows : (c + 1) * rows, :] = low


def gather_cells(sz, table, ids, out):
    for j in range(sz.kn):
        got = gather_chunk(table, row_of(ids, j), row_of(ids, sz.kn + j), 3, sz.rows)
        for c in range(3):
            out[c * sz.kn + j : c * sz.kn + j + 1, :] = got[c]


def scatter_sets(sz, parts, sets, ids, acc):
    group = math.gcd(sz.np, 4)
    low_rows = 3 * sz.wp

    def some(t):
        total = None
        for s in range(group):
            one, index = sets.at[t * group + s], ids.at[t * group + s]
            for j in range(sz.kn):
                values = [row_of(one, c * sz.kn + j) for c in range(parts)]
                terms = scatter_chunk(
                    values, row_of(index, j), row_of(index, sz.kn + j), sz.wp, parts - 3
                )
                total = added(total, terms)
        return total

    if group == sz.np:
        high, low = some(0)
        acc[...] = high
        acc[0:low_rows, :] += low
    else:
        acc[...] = jnp.zeros_like(acc)

        def body(t, carry):
            high, low = some(t)
            acc[...] += high
            acc[0:low_rows, :] += low
            return carry

        lax.fori_loop(0, sz.np // group, body, 0)


def sort_sets(sz, plan, own, got, sets, rows, offset):
    a, b, others = got
    index = [plan, lax.rem(plan + 1 - 2 * (plan % 2) + sz.np, sz.np), partner_b(plan, sz.np)]
    sets[index[1]] = a[offset : offset + rows, :]
    sets[index[2]] = b[offset : offset + rows, :]
    for shift, ref in zip(range(2, sz.np - 1), others):
        sets[lax.rem(plan + sz.np - shift, sz.np)] = ref[...]
    sets[index[0]] = own[...]


def send_sums(sz, depth, parts, acc, to_da, to_db, offset):
    even = depth % 2 == 0
    pr = sz.pr
    for c in range(parts):
        first = acc[c * sz.wp : c * sz.wp + pr, :]
        last = acc[c * sz.wp + 2 * pr : c * sz.wp + 3 * pr, :]
        to_da[offset + c * pr : offset + (c + 1) * pr, :] = jnp.where(even, last, first)
        to_db[offset + c * pr : offset + (c + 1) * pr, :] = jnp.where(even, first, last)


def total_sum(sz, depth, c, acc, from_da, from_db, offset):
    rows = slice(offset + c * sz.pr, offset + (c + 1) * sz.pr)
    low, high = low_high(depth, sz.nd, from_da, from_db, (rows, slice(None)))
    return low + acc[c * sz.wp + sz.pr : c * sz.wp + 2 * sz.pr, :] + high


def move_pile(sz, depth, pile, jack, mass, count, acc, from_da, from_db, offset, out):
    for c in range(3):
        rows = slice(c * sz.pr, (c + 1) * sz.pr)
        summed = total_sum(sz, depth, c, acc, from_da, from_db, offset)
        p = pile[rows, :]
        out[rows, :] = p + time_step * (jack[rows, :] - (count[...] * p - summed)) / mass[...]


def new_stress(along_z, along_x, along_y, old, flag):
    normal = [along_z[0], along_x[1], along_y[2]]
    shear = [along_x[0] + along_z[1], along_y[0] + along_z[2], along_y[1] + along_x[2]]
    bulk = (0.5 * time_step) * (normal[0] + normal[1] + normal[2])
    trial = [old[c] + (time_step * normal[c] + bulk) for c in range(3)]
    sheared = [old[3 + c] + (0.5 * time_step) * shear[c] for c in range(3)]
    pressure = (trial[0] + trial[1] + trial[2]) * (1.0 / 3.0)
    dev = [t - pressure for t in trial]
    second = 0.5 * (dev[0] * dev[0] + dev[1] * dev[1] + dev[2] * dev[2])
    for t in sheared:
        second = second + t * t
    shrink = 1.0 / (1.0 + cone_rate * jnp.sqrt(second))
    factor = jnp.where(flag == 1, shrink, 0.0)
    elastic = flag == 0
    return [jnp.where(elastic, t, d * factor + pressure) for t, d in zip(trial, dev)] + [
        jnp.where(elastic, t, t * factor) for t in sheared
    ]


def taker(refs):
    refs = list(refs)
    return lambda n: [refs.pop(0) for _ in range(n)]


def first_kernel(sz, *refs):
    take = taker(refs)
    sources = take(9)
    to_da, to_db, to_pa, to_pb, to_all, cell_ids, elem_ids, pile, mass, jack = take(10)
    stress, velocity, density, flags = take(4)
    high, low, pile_in, mass_in, jack_in, elem_in, cell_in, sems = take(8)
    targets = (
        cell_in, velocity, elem_in, pile_in, mass_in, jack_in, stress, flags, density,
    )
    copies = [
        pltpu.make_async_copy(a, b, sems.at[i]) for i, (a, b) in enumerate(zip(sources, targets))
    ]
    for copy in copies:
        copy.start()
    depth, plan = lax.axis_index("depth"), lax.axis_index("plan")
    kn, pr, cx, cz = sz.kn, sz.pr, sz.cx, sz.cz
    for copy in copies[:3]:
        copy.wait()
    for j in range(kn):
        lanes = slice(j * COLS, (j + 1) * COLS)
        cell, elem = cell_in[:, lanes], elem_in[:, lanes]
        cell_ids[j : j + 1, :] = lax.shift_right_arithmetic(cell, 8)
        cell_ids[kn + j : kn + j + 1, :] = lax.bitwise_and(cell, COLS - 1)
        elem_ids[j : j + 1, :] = lax.shift_right_arithmetic(elem, 8)
        elem_ids[kn + j : kn + j + 1, :] = lax.bitwise_and(elem, COLS - 1)
        to_all[3 * kn + j : 3 * kn + j + 1, :] = jnp.where(cell >= 0, elem, -1).astype(F32)
    store_split(sz, lambda c: velocity[c], 3, sz.rows, (high, low))
    gather_cells(sz, (high, low), cell_ids, to_all)
    for copy in copies[3:]:
        copy.wait()
    for r in range(pr):
        lanes = slice(r * COLS, (r + 1) * COLS)
        for c in range(3):
            pile[c * pr + r : c * pr + r + 1, :] = pile_in[c : c + 1, lanes]
            jack[c * pr + r : c * pr + r + 1, :] = jack_in[c : c + 1, lanes]
        mass[r : r + 1, :] = mass_in[:, lanes]
    to_da[3 * cx :, :] = pile[...]
    to_db[3 * cx :, :] = pile[...]
    to_pa[7 * cz :, :] = to_all[...]
    to_pb[7 * cz :, :] = to_all[...]
    plane = lambda c, z: stress[c, z * cx : (z + 1) * cx, :]
    send_layers(sz, depth, DEPTH_PART, plane, to_da, to_db)
    columns = [(column(sz, stress, c, 0), column(sz, stress, c, cx - 1)) for c in range(6)]
    ends = [
        jnp.concatenate([row_of(flags, z * cx + x) for z in range(cz)], axis=0).astype(F32)
        for x in (0, cx - 1)
    ]
    send_columns(sz, plan, columns + [ends], to_pa, to_pb)


def update_velocity(
    sz, depth, stress, velocity, density, from_da, from_db, columns, window_of, at_cells,
    cell_ids, elem_ids, out, high, low, on_cells,
):
    kn, rows, wp, cx, cz = sz.kn, sz.rows, sz.wp, sz.cx, sz.cz
    pile_high, pile_low = high.at[0 : 3 * wp, :], low.at[0 : 3 * wp, :]
    store_split(
        sz, lambda c: jnp.concatenate(list(window_of(c)), axis=0), 3, wp, (pile_high, pile_low)
    )
    total = None
    for j in range(kn):
        at_pile = gather_chunk(
            (pile_high, pile_low), row_of(elem_ids, j), row_of(elem_ids, kn + j), 3, wp
        )
        push = [at_pile[c] - row_of(at_cells, c * kn + j) for c in range(3)]
        total = added(
            total, scatter_chunk(push, row_of(cell_ids, j), row_of(cell_ids, kn + j), rows)
        )
    on_cells[...] = total[0] + total[1]
    plane = lambda c, z: stress[c, z * cx : (z + 1) * cx, :]
    d_low, d_high = low_high(
        depth, sz.nd, from_da, from_db, (slice(0, 3 * cx), slice(None))
    )
    for z in range(cz):
        here = slice(z * cx, (z + 1) * cx)
        scale = time_step / density[here, :]
        for i in range(3):
            ahead = plane(DEPTH_PART[i], z + 1) if z + 1 < cz else d_high[i * cx : (i + 1) * cx]
            behind = plane(DEPTH_PART[i], z - 1) if z > 0 else d_low[i * cx : (i + 1) * cx]
            c = PLAN_PART[i]
            twice = (
                (ahead - behind)
                + shifted_rows(
                    plane(c, z), row_of(columns, c * cz + z), row_of(columns, (6 + c) * cz + z)
                )
                + shifted_lanes(plane(LAST_PART[i], z))
            )
            force = 0.5 * twice + on_cells[i * rows + z * cx : i * rows + (z + 1) * cx, :]
            out[i, here, :] = velocity[i, here, :] + scale * force


def update_columns(
    sz, depth, plan, velocity, from_pa, from_pb, from_da, from_db, offset, old, flags, out
):
    cz, cx = sz.cz, sz.cx
    lines = low_high(depth, sz.nd, from_da, from_db, (slice(offset, offset + 8), slice(None)))
    strips = low_high(plan, sz.np, from_pa, from_pb, (slice(0, 6 * cz), slice(None)))
    inside = plan > 0, plan < sz.np - 1
    for side in range(2):
        along_z, along_x, along_y = [], [], []
        for c in range(3):
            near = strips[side][c * cz : (c + 1) * cz]
            away = strips[side][(3 + c) * cz : (4 + c) * cz]
            mine = column(sz, velocity, c, 0 if side == 0 else cx - 1)
            line = slice(side * 3 + c, side * 3 + c + 1)
            along_z.append(shifted_rows(near, lines[0][line], lines[1][line]))
            along_x.append(mine - away if side == 0 else away - mine)
            along_y.append(shifted_lanes(near))
        where = lambda c: slice((side * 6 + c) * cz, (side * 6 + c + 1) * cz)
        flag = flags[side * cz : (side + 1) * cz, :]
        got = new_stress(along_z, along_x, along_y, [old[where(c), :] for c in range(6)], flag)
        for c in range(6):
            out[where(c), :] = jnp.where(inside[side], got[c], jnp.zeros_like(got[c]))


def update_stress(
    sz, depth, plan, stress, velocity, flags, from_da, from_db, from_pa, from_pb, out,
    plane_done=None,
):
    cx, cz = sz.cx, sz.cz
    plane = lambda c, z: velocity[c, z * cx : (z + 1) * cx, :]
    d_low, d_high = low_high(
        depth, sz.nd, from_da, from_db, (slice(0, 3 * cx), slice(None))
    )
    p_low, p_high = low_high(plan, sz.np, from_pa, from_pb, (slice(0, 3 * cz), slice(None)))
    for z in range(cz):
        here = slice(z * cx, (z + 1) * cx)
        v = [plane(c, z) for c in range(3)]
        along_z, along_x = [], []
        for c in range(3):
            ahead = plane(c, z + 1) if z + 1 < cz else d_high[c * cx : (c + 1) * cx]
            behind = plane(c, z - 1) if z > 0 else d_low[c * cx : (c + 1) * cx]
            along_z.append(ahead - behind)
            row = slice(c * cz + z, c * cz + z + 1)
            along_x.append(shifted_rows(v[c], p_low[row], p_high[row]))
        along_y = [shifted_lanes(v[c]) for c in range(3)]
        got = new_stress(
            along_z, along_x, along_y, [stress[c, here, :] for c in range(6)], flags[here, :]
        )
        for c in range(6):
            out[c, here, :] = got[c]
        if plane_done is not None:
            plane_done(z)
    return p_low, p_high


def window_from(sz, depth, pile, from_da, from_db, offset):
    def of(c):
        rows = slice(offset + c * sz.pr, offset + (c + 1) * sz.pr)
        low, high = low_high(depth, sz.nd, from_da, from_db, (rows, slice(None)))
        return low, pile[c * sz.pr : (c + 1) * sz.pr, :], high

    return of


def velocity_kernel(sz, step, *refs):
    depth, plan = lax.axis_index("depth"), lax.axis_index("plan")
    take = taker(refs)
    cx, cz = sz.cx, sz.cz
    stress, velocity, density, cell_ids, elem_ids, at_cells, pile = take(7)
    from_da, from_db, from_pa, from_pb = take(4)
    if step > 0:
        old_columns, column_flags, acc = take(3)
    out, to_da, to_db, to_pa, to_pb = take(5)
    if step < STEPS - 1:
        to_all, columns = take(2)
    if step == 0:
        (column_flags,) = take(1)
    if step == STEPS - 1:
        (columns,) = take(1)
    high, low, on_cells = take(3)
    head = 3 * cx
    if step == 0:
        offset = head
        strips = low_high(plan, sz.np, from_pa, from_pb, (slice(0, 7 * cz), slice(None)))
        for side in range(2):
            columns[6 * cz * side : 6 * cz * (side + 1), :] = strips[side][0 : 6 * cz]
            column_flags[cz * side : cz * (side + 1), :] = strips[side][6 * cz :].astype(I32)
    else:
        offset = head + 8
        update_columns(
            sz, depth, plan, velocity, from_pa, from_pb, from_da, from_db, head, old_columns,
            column_flags, columns,
        )
    update_velocity(
        sz, depth, stress, velocity, density, from_da, from_db, columns,
        window_from(sz, depth, pile, from_da, from_db, offset), at_cells, cell_ids, elem_ids,
        out, high, low, on_cells,
    )
    plane = lambda c, z: out[c, z * cx : (z + 1) * cx, :]
    send_layers(sz, depth, range(3), plane, to_da, to_db)
    if step > 0:
        send_sums(sz, depth, 3, acc, to_da, to_db, head)
    shifts = range(2 if step < STEPS - 1 else 1)
    ends = [
        (column(sz, out, c, x), column(sz, out, c, cx - 1 - x)) for x in shifts for c in range(3)
    ]
    send_columns(sz, plan, ends, to_pa, to_pb)
    if step < STEPS - 1:
        store_split(sz, lambda c: out[c], 3, sz.rows, (high, low))
        gather_cells(sz, (high, low), cell_ids, to_all)
        to_pa[6 * cz :, :] = to_all[...]
        to_pb[6 * cz :, :] = to_all[...]


def sums_kernel(sz, step, *refs):
    depth, plan = lax.axis_index("depth"), lax.axis_index("plan")
    take = taker(refs)
    own, from_pa, from_pb = take(3)
    from_others = take(max(sz.np - 3, 0))
    kn, head = sz.kn, 3 * sz.cx
    if step == 0:
        layer_a, layer_b, to_da, to_db, acc, set_ids, sets = take(7)
        sort_sets(sz, plan, own, (from_pa, from_pb, from_others), sets, 4 * kn, 7 * sz.cz)
        for s in range(sz.np):
            ids = sets[s, 3 * kn : 4 * kn, :]
            elem = ids.astype(I32)
            set_ids[s, 0:kn, :] = lax.shift_right_arithmetic(elem, 8)
            set_ids[s, kn : 2 * kn, :] = lax.bitwise_and(elem, COLS - 1)
            sets[s, 3 * kn : 4 * kn, :] = jnp.where(ids >= 0, 1.0, 0.0)
        scatter_sets(sz, 4, sets, set_ids, acc)
        to_da[0:head, :] = layer_a[...]
        to_db[0:head, :] = layer_b[...]
        send_sums(sz, depth, 4, acc, to_da, to_db, head)
    else:
        set_ids, acc, sets = take(3)
        sort_sets(sz, plan, own, (from_pa, from_pb, from_others), sets, 3 * kn, 6 * sz.cz)
        scatter_sets(sz, 3, sets, set_ids, acc)


def stress_kernel(sz, step, *refs):
    depth, plan = lax.axis_index("depth"), lax.axis_index("plan")
    take = taker(refs)
    stress, velocity, flags, from_da, from_db, from_pa, from_pb = take(7)
    pile, mass, jack, acc = take(4)
    cx, cz, head = sz.cx, sz.cz, 3 * sz.cx
    froms = from_da, from_db, from_pa, from_pb
    if step == 0:
        out, to_da, to_db, new_pile, count = take(5)
        count[...] = total_sum(sz, depth, 3, acc, from_da, from_db, head)
    elif step < STEPS - 1:
        count, out, to_da, to_db, new_pile = take(5)
    else:
        count, stress_out, velocity_out, pile_out, out, new_pile, flat_pile, sems = take(8)
        copies = [pltpu.make_async_copy(velocity, velocity_out, sems.at[cz])]
        copies[0].start()
    move_pile(sz, depth, pile, jack, mass, count, acc, from_da, from_db, head, new_pile)
    if step < STEPS - 1:
        strips = update_stress(sz, depth, plan, stress, velocity, flags, *froms, out)
        plane = lambda c, z: out[c, z * cx : (z + 1) * cx, :]
        send_layers(sz, depth, DEPTH_PART, plane, to_da, to_db)
        lines = [
            [strips[side][c * cz + z : c * cz + z + 1] for side in range(2) for c in range(3)]
            for z in (0, cz - 1)
        ]
        blank = [jnp.zeros((2, sz.cy), F32)]
        first, last = [jnp.concatenate(one + blank, axis=0) for one in lines]
        even = depth % 2 == 0
        to_da[head : head + 8, :] = jnp.where(even, last, first)
        to_db[head : head + 8, :] = jnp.where(even, first, last)
        to_da[head + 8 :, :] = new_pile[...]
        to_db[head + 8 :, :] = new_pile[...]
        return
    for r in range(sz.pr):
        for c in range(3):
            row = c * sz.pr + r
            flat_pile[c : c + 1, r * COLS : (r + 1) * COLS] = new_pile[row : row + 1, :]
    copies.append(pltpu.make_async_copy(flat_pile, pile_out, sems.at[cz + 1]))
    copies[-1].start()

    def plane_done(z):
        part = (slice(None), pl.ds(z * cx, cx), slice(None))
        copies.append(pltpu.make_async_copy(out.at[part], stress_out.at[part], sems.at[z]))
        copies[-1].start()

    update_stress(sz, depth, plan, stress, velocity, flags, *froms, out, plane_done)
    for copy in copies:
        copy.wait()


def call(body, name, ins, outs, scratch=(), copies=0, far_ins=False, far_outs=False, flops=0):
    vmem, far = pl.BlockSpec(memory_space=pltpu.VMEM), pl.BlockSpec(memory_space=pl.ANY)
    sems = [pltpu.SemaphoreType.DMA((copies,))] if copies else []
    moved = sum(4 * x.size for x in ins) + sum(4 * math.prod(shape) for shape, _ in outs)
    return pl.pallas_call(
        body,
        out_shape=[jax.ShapeDtypeStruct(shape, dtype) for shape, dtype in outs],
        in_specs=[far if far_ins else vmem] * len(ins),
        out_specs=[far if far_outs else vmem] * len(outs),
        scratch_shapes=[pltpu.VMEM(shape, dtype) for shape, dtype in scratch] + sems,
        compiler_params=pltpu.CompilerParams(vmem_limit_bytes=48 * 2**20),
        cost_estimate=pl.CostEstimate(flops=flops, bytes_accessed=moved, transcendentals=0),
        name=name,
    )(*[pltpu.with_memory_space_constraint(x, pltpu.HBM) if far_ins else x for x in ins])


def matchings(count):
    first = [(i, i ^ 1) for i in range(count)]
    second = [(i, (i - 1) % count if i % 2 == 0 else (i + 1) % count) for i in range(count)]
    return first, second


def shards(
    stress, velocity, density, flags, pile_velocity, pile_mass, jack_force, pair_elem, pair_cell
):
    sz = Sizes(stress, pile_velocity, pair_cell)
    cz, cx, cy, rows, kn, pr = sz.cz, sz.cx, sz.cy, sz.rows, sz.kn, sz.pr
    assert cy == COLS and sz.pile % COLS == 0 and sz.pairs % COLS == 0
    assert sz.nd % 2 == 0 and sz.np % 2 == 0
    d_first, d_second = matchings(sz.nd)
    p_first, p_second = matchings(sz.np)

    def swap_plan(pa, pb):
        pb = lax.ppermute(pb, "plan", p_second)
        pa = lax.ppermute(pa, "plan", p_first)
        return [pa, pb]

    def swap_depth(da, db):
        db = lax.ppermute(db, "depth", d_second)
        da = lax.ppermute(da, "depth", d_first)
        return [da, db]

    def to_others(x):
        shifts = range(2, sz.np - 1)
        return [
            lax.ppermute(x, "plan", [(i, (i + s) % sz.np) for i in range(sz.np)]) for s in shifts
        ]

    full_shape = stress.shape, velocity.shape
    stress = stress.reshape(6, rows, cy)
    velocity = velocity.reshape(3, rows, cy)
    density = density.reshape(rows, cy)
    flags = flags.reshape(rows, cy)
    pr3, wp = 3 * pr, sz.wp
    tables = [((max(3 * rows, 3 * wp), COLS), BF16)] * 2
    cells = [((3 * rows, COLS), F32)]
    scatter = 4 * 3 * wp * COLS * sz.pairs * sz.np
    layers = lambda extra: [((3 * cx + extra, COLS), F32)] * 2
    strips = lambda extra: [((extra, COLS), F32)] * 2

    to = call(
        functools.partial(first_kernel, sz),
        "first",
        [
            pair_cell, velocity, pair_elem, pile_velocity, pile_mass.reshape(1, -1), jack_force,
            stress, flags, density,
        ],
        layers(pr3)
        + strips(7 * cz + 4 * kn)
        + [
            ((4 * kn, COLS), F32), ((2 * kn, COLS), I32), ((2 * kn, COLS), I32),
            ((pr3, COLS), F32), ((pr, COLS), F32), ((pr3, COLS), F32),
            (stress.shape, F32), (velocity.shape, F32), (density.shape, F32), (flags.shape, I32),
        ],
        tables
        + [(pile_velocity.shape, F32), ((1, sz.pile), F32), (jack_force.shape, F32)]
        + [(pair_elem.shape, I32), (pair_cell.shape, I32)],
        copies=9,
        far_ins=True,
    )
    at_cells, cell_ids, elem_ids, pile, mass, jack = to[4:10]
    stress, velocity, density, flags = to[10:]
    others = to_others(at_cells)
    by_plan = swap_plan(*to[2:4])
    by_depth = swap_depth(*to[0:2])
    count = acc = set_ids = columns = column_flags = None
    for step in range(STEPS):
        last = step == STEPS - 1
        state = [] if step == 0 else [columns, column_flags, acc]
        moved = call(
            functools.partial(velocity_kernel, sz, step),
            f"velocity_{step}",
            [stress, velocity, density, cell_ids, elem_ids, at_cells, pile]
            + by_depth
            + by_plan
            + state,
            [(velocity.shape, F32)]
            + layers(0 if step == 0 else pr3)
            + strips(3 * cz if last else 6 * cz + 3 * kn)
            + ([] if last else [((3 * kn, COLS), F32), ((12 * cz, COLS), F32)])
            + ([((2 * cz, COLS), I32)] if step == 0 else []),
            ([((12 * cz, COLS), F32)] if last else []) + tables + cells,
        )
        velocity, layer = moved[0], list(moved[1:3])
        sets = [at_cells, *by_plan, *others]
        if not last:
            at_cells, columns = moved[5:7]
            others = to_others(at_cells)
        by_plan = swap_plan(*moved[3:5])
        if step == 0:
            column_flags = moved[7]
            *layer, acc, set_ids = call(
                functools.partial(sums_kernel, sz, 0),
                "sums_0",
                sets + layer,
                layers(4 * pr)
                + [((4 * wp, COLS), F32), ((sz.np, 2 * kn, COLS), I32)],
                [((sz.np, 4 * kn, COLS), F32)],
                flops=scatter,
            )
        by_depth = swap_depth(*layer)
        ins = [stress, velocity, flags, *by_depth, *by_plan, pile, mass, jack, acc]
        ins = ins if step == 0 else ins + [count]
        if last:
            stress, velocity, pile = call(
                functools.partial(stress_kernel, sz, step),
                f"stress_{step}",
                ins,
                [(stress.shape, F32), (velocity.shape, F32), (pile_velocity.shape, F32)],
                [(stress.shape, F32), ((pr3, COLS), F32), (pile_velocity.shape, F32)],
                copies=cz + 2,
                far_outs=True,
            )
            break
        got = call(
            functools.partial(stress_kernel, sz, step),
            f"stress_{step}",
            ins,
            [(stress.shape, F32)]
            + layers(8 + pr3)
            + [((pr3, COLS), F32)]
            + ([((pr, COLS), F32)] if step == 0 else []),
        )
        stress, pile = got[0], got[3]
        count = got[4] if step == 0 else count
        by_depth = swap_depth(*got[1:3])
        (acc,) = call(
            functools.partial(sums_kernel, sz, step + 1),
            f"sums_{step + 1}",
            [at_cells, *by_plan, *others, set_ids],
            [((3 * wp, COLS), F32)],
            [((sz.np, 3 * kn, COLS), F32)],
            flops=scatter,
        )
    return stress.reshape(full_shape[0]), velocity.reshape(full_shape[1]), pile


def solution(mesh):
    cells, field = P("depth", "plan", None), P(None, "depth", "plan", None)
    pile, pairs = P(None, "depth"), P("depth", "plan")
    return jax.shard_map(
        shards,
        mesh=mesh,
        in_specs=(field, field, cells, cells, pile, P("depth"), pile, pairs, pairs),
        out_specs=(field, field, pile),
        check_vma=False,
    )
```

```python
import functools
import math

import jax
import jax.numpy as jnp
from jax import lax
from jax.experimental import pallas as pl
from jax.experimental.pallas import tpu as pltpu
from jax.sharding import PartitionSpec as P


STEPS = 3
time_step = 0.2
cone_rate = 1.5
F32, BF16, I32 = jnp.float32, jnp.bfloat16, jnp.int32
COLS = 256
DEPTH_PART = (0, 3, 4)
PLAN_PART = (3, 1, 5)
LAST_PART = (4, 5, 2)


class Sizes:
    def __init__(self, stress, pile_velocity, pair_cell):
        self.cz, self.cx, self.cy = stress.shape[1:]
        self.rows = self.cz * self.cx
        self.pile = pile_velocity.shape[1]
        self.pr = self.pile // COLS
        self.wp = 3 * self.pr
        self.pairs = pair_cell.shape[1]
        self.kn = self.pairs // COLS
        self.nd = lax.axis_size("depth")
        self.np = lax.axis_size("plan")


def partner_b(index, count):
    return jnp.where(
        index % 2 == 0, lax.rem(index + count - 1, count), lax.rem(index + 1, count)
    )


def low_high(index, count, ref_a, ref_b, where):
    a, b = ref_a[where], ref_b[where]
    even = index % 2 == 0
    zero = jnp.zeros_like(a)
    low = jnp.where(index > 0, jnp.where(even, b, a), zero)
    high = jnp.where(index < count - 1, jnp.where(even, a, b), zero)
    return low, high


def split(x):
    high = x.astype(BF16)
    return high, (x - high.astype(F32)).astype(BF16)


def hits(ids, count):
    return lax.broadcasted_iota(I32, (count, ids.shape[1]), 0) == ids


def one_hot(ids, count):
    return jnp.where(hits(ids, count), 1.0, 0.0).astype(BF16)


def gather_chunk(table, row_ids, col_ids, parts, rows):
    pick = one_hot(col_ids, COLS)
    got = jnp.dot(table[0][...], pick, preferred_element_type=F32)
    got = got + jnp.dot(table[1][...], pick, preferred_element_type=F32)
    mask = hits(row_ids, rows)
    return [
        jnp.sum(jnp.where(mask, got[c * rows : (c + 1) * rows], 0.0), axis=0, keepdims=True)
        for c in range(parts)
    ]


def scatter_chunk(values, row_ids, col_ids, rows, exact=0):
    put = one_hot(col_ids, COLS)
    mask = hits(row_ids, rows)
    pairs = [split(v) for v in values]
    pieces = [v[0] for v in pairs], [v[1] for v in pairs[: len(values) - exact]]
    terms = []
    for piece in pieces:
        spread = jnp.concatenate(
            [jnp.where(mask, v.astype(F32), 0.0) for v in piece], axis=0
        ).astype(BF16)
        terms.append(
            lax.dot_general(spread, put, (((1,), (1,)), ((), ())), preferred_element_type=F32)
        )
    return terms


def added(total, terms):
    return terms if total is None else [a + b for a, b in zip(total, terms)]


def row_of(ref, row):
    return ref[row : row + 1, :]


def shifted_rows(a, low, high):
    count = a.shape[0]
    row = lax.broadcasted_iota(I32, a.shape, 0)
    up = jnp.where(row == count - 1, high, pltpu.roll(a, count - 1, 0))
    down = jnp.where(row == 0, low, pltpu.roll(a, 1, 0))
    return up - down


def shifted_lanes(a):
    count = a.shape[1]
    lane = lax.broadcasted_iota(I32, a.shape, 1)
    up = jnp.where(lane == count - 1, 0.0, pltpu.roll(a, count - 1, 1))
    down = jnp.where(lane == 0, 0.0, pltpu.roll(a, 1, 1))
    return up - down


def send_layers(sz, depth, parts, plane, to_da, to_db):
    even, cx = depth % 2 == 0, sz.cx
    for i, c in enumerate(parts):
        first, last = plane(c, 0), plane(c, sz.cz - 1)
        to_da[i * cx : (i + 1) * cx, :] = jnp.where(even, last, first)
        to_db[i * cx : (i + 1) * cx, :] = jnp.where(even, first, last)


def column(sz, ref, c, x):
    rows = [z * sz.cx + x for z in range(sz.cz)]
    return jnp.concatenate([ref[c, r : r + 1, :] for r in rows], axis=0)


def send_columns(sz, plan, columns, to_pa, to_pb):
    even, cz = plan % 2 == 0, sz.cz
    for i, (first, last) in enumerate(columns):
        to_pa[i * cz : (i + 1) * cz, :] = jnp.where(even, last, first)
        to_pb[i * cz : (i + 1) * cz, :] = jnp.where(even, first, last)


def store_split(source, parts, rows, refs):
    for c in range(parts):
        high, low = split(source(c))
        refs[0][c * rows : (c + 1) * rows, :] = high
        refs[1][c * rows : (c + 1) * rows, :] = low


def gather_cells(sz, table, ids, out):
    for j in range(sz.kn):
        got = gather_chunk(table, row_of(ids, j), row_of(ids, sz.kn + j), 3, sz.rows)
        for c in range(3):
            out[c * sz.kn + j : c * sz.kn + j + 1, :] = got[c]


def scatter_sets(sz, parts, sets, ids, acc):
    group = math.gcd(sz.np, 4)
    low_rows = 3 * sz.wp

    def some(t):
        total = None
        for s in range(group):
            one, index = sets.at[t * group + s], ids.at[t * group + s]
            for j in range(sz.kn):
                values = [row_of(one, c * sz.kn + j) for c in range(parts)]
                terms = scatter_chunk(
                    values, row_of(index, j), row_of(index, sz.kn + j), sz.wp, parts - 3
                )
                total = added(total, terms)
        return total

    if group == sz.np:
        high, low = some(0)
        acc[...] = high
        acc[0:low_rows, :] += low
    else:
        acc[...] = jnp.zeros_like(acc)

        def body(t, carry):
            high, low = some(t)
            acc[...] += high
            acc[0:low_rows, :] += low
            return carry

        lax.fori_loop(0, sz.np // group, body, 0)


def sort_sets(sz, plan, own, got, sets, rows, offset):
    a, b, others = got
    index = [plan, lax.rem(plan + 1 - 2 * (plan % 2) + sz.np, sz.np), partner_b(plan, sz.np)]
    sets[index[1]] = a[offset : offset + rows, :]
    sets[index[2]] = b[offset : offset + rows, :]
    for shift, ref in zip(range(2, sz.np - 1), others):
        sets[lax.rem(plan + sz.np - shift, sz.np)] = ref[...]
    sets[index[0]] = own[...]


def send_sums(sz, depth, parts, acc, to_da, to_db, offset):
    even = depth % 2 == 0
    pr = sz.pr
    for c in range(parts):
        first = acc[c * sz.wp : c * sz.wp + pr, :]
        last = acc[c * sz.wp + 2 * pr : c * sz.wp + 3 * pr, :]
        to_da[offset + c * pr : offset + (c + 1) * pr, :] = jnp.where(even, last, first)
        to_db[offset + c * pr : offset + (c + 1) * pr, :] = jnp.where(even, first, last)


def total_sum(sz, depth, c, acc, from_da, from_db, offset):
    rows = slice(offset + c * sz.pr, offset + (c + 1) * sz.pr)
    low, high = low_high(depth, sz.nd, from_da, from_db, (rows, slice(None)))
    return low + acc[c * sz.wp + sz.pr : c * sz.wp + 2 * sz.pr, :] + high


def move_pile(sz, depth, pile, jack, mass, count, acc, from_da, from_db, offset, out):
    for c in range(3):
        rows = slice(c * sz.pr, (c + 1) * sz.pr)
        summed = total_sum(sz, depth, c, acc, from_da, from_db, offset)
        p = pile[rows, :]
        out[rows, :] = p + time_step * (jack[rows, :] - (count[...] * p - summed)) / mass[...]


def new_stress(along_z, along_x, along_y, old, flag):
    normal = [along_z[0], along_x[1], along_y[2]]
    shear = [along_x[0] + along_z[1], along_y[0] + along_z[2], along_y[1] + along_x[2]]
    bulk = (0.5 * time_step) * (normal[0] + normal[1] + normal[2])
    trial = [old[c] + (time_step * normal[c] + bulk) for c in range(3)]
    sheared = [old[3 + c] + (0.5 * time_step) * shear[c] for c in range(3)]
    pressure = (trial[0] + trial[1] + trial[2]) * (1.0 / 3.0)
    dev = [t - pressure for t in trial]
    second = 0.5 * (dev[0] * dev[0] + dev[1] * dev[1] + dev[2] * dev[2])
    for t in sheared:
        second = second + t * t
    shrink = 1.0 / (1.0 + cone_rate * jnp.sqrt(second))
    factor = jnp.where(flag == 1, shrink, 0.0)
    elastic = flag == 0
    return [jnp.where(elastic, t, d * factor + pressure) for t, d in zip(trial, dev)] + [
        jnp.where(elastic, t, t * factor) for t in sheared
    ]


def taker(refs):
    refs = list(refs)
    return lambda n: [refs.pop(0) for _ in range(n)]


def first_kernel(sz, *refs):
    take = taker(refs)
    sources = take(9)
    to_da, to_db, to_pa, to_pb, to_all, cell_ids, elem_ids, pile, mass, jack = take(10)
    stress, velocity, density, flags = take(4)
    high, low, pile_in, mass_in, jack_in, elem_in, cell_in, sems = take(8)
    targets = (
        cell_in, velocity, elem_in, pile_in, mass_in, jack_in, stress, flags, density,
    )
    copies = [
        pltpu.make_async_copy(a, b, sems.at[i]) for i, (a, b) in enumerate(zip(sources, targets))
    ]
    for copy in copies:
        copy.start()
    depth, plan = lax.axis_index("depth"), lax.axis_index("plan")
    kn, pr, cx, cz = sz.kn, sz.pr, sz.cx, sz.cz
    for copy in copies[:3]:
        copy.wait()
    for j in range(kn):
        lanes = slice(j * COLS, (j + 1) * COLS)
        cell, elem = cell_in[:, lanes], elem_in[:, lanes]
        cell_ids[j : j + 1, :] = lax.shift_right_arithmetic(cell, 8)
        cell_ids[kn + j : kn + j + 1, :] = lax.bitwise_and(cell, COLS - 1)
        elem_ids[j : j + 1, :] = lax.shift_right_arithmetic(elem, 8)
        elem_ids[kn + j : kn + j + 1, :] = lax.bitwise_and(elem, COLS - 1)
        to_all[3 * kn + j : 3 * kn + j + 1, :] = jnp.where(cell >= 0, elem, -1).astype(F32)
    store_split(lambda c: velocity[c], 3, sz.rows, (high, low))
    gather_cells(sz, (high, low), cell_ids, to_all)
    for copy in copies[3:]:
        copy.wait()
    for r in range(pr):
        lanes = slice(r * COLS, (r + 1) * COLS)
        for c in range(3):
            pile[c * pr + r : c * pr + r + 1, :] = pile_in[c : c + 1, lanes]
            jack[c * pr + r : c * pr + r + 1, :] = jack_in[c : c + 1, lanes]
        mass[r : r + 1, :] = mass_in[:, lanes]
    to_da[3 * cx :, :] = pile[...]
    to_db[3 * cx :, :] = pile[...]
    to_pa[7 * cz :, :] = to_all[...]
    to_pb[7 * cz :, :] = to_all[...]
    plane = lambda c, z: stress[c, z * cx : (z + 1) * cx, :]
    send_layers(sz, depth, DEPTH_PART, plane, to_da, to_db)
    columns = [(column(sz, stress, c, 0), column(sz, stress, c, cx - 1)) for c in range(6)]
    ends = [
        jnp.concatenate([row_of(flags, z * cx + x) for z in range(cz)], axis=0).astype(F32)
        for x in (0, cx - 1)
    ]
    send_columns(sz, plan, columns + [ends], to_pa, to_pb)


def update_velocity(
    sz, depth, stress, velocity, density, from_da, from_db, columns, window_of, at_cells,
    cell_ids, elem_ids, out, high, low, on_cells,
):
    kn, rows, wp, cx, cz = sz.kn, sz.rows, sz.wp, sz.cx, sz.cz
    pile_high, pile_low = high.at[0 : 3 * wp, :], low.at[0 : 3 * wp, :]
    store_split(lambda c: jnp.concatenate(list(window_of(c)), axis=0), 3, wp, (pile_high, pile_low))
    total = None
    for j in range(kn):
        at_pile = gather_chunk(
            (pile_high, pile_low), row_of(elem_ids, j), row_of(elem_ids, kn + j), 3, wp
        )
        push = [at_pile[c] - row_of(at_cells, c * kn + j) for c in range(3)]
        total = added(
            total, scatter_chunk(push, row_of(cell_ids, j), row_of(cell_ids, kn + j), rows)
        )
    on_cells[...] = total[0] + total[1]
    plane = lambda c, z: stress[c, z * cx : (z + 1) * cx, :]
    d_low, d_high = low_high(
        depth, sz.nd, from_da, from_db, (slice(0, 3 * cx), slice(None))
    )
    for z in range(cz):
        here = slice(z * cx, (z + 1) * cx)
        scale = time_step / density[here, :]
        for i in range(3):
            ahead = plane(DEPTH_PART[i], z + 1) if z + 1 < cz else d_high[i * cx : (i + 1) * cx]
            behind = plane(DEPTH_PART[i], z - 1) if z > 0 else d_low[i * cx : (i + 1) * cx]
            c = PLAN_PART[i]
            twice = (
                (ahead - behind)
                + shifted_rows(
                    plane(c, z), row_of(columns, c * cz + z), row_of(columns, (6 + c) * cz + z)
                )
                + shifted_lanes(plane(LAST_PART[i], z))
            )
            force = 0.5 * twice + on_cells[i * rows + z * cx : i * rows + (z + 1) * cx, :]
            out[i, here, :] = velocity[i, here, :] + scale * force


def update_columns(
    sz, depth, plan, velocity, from_pa, from_pb, from_da, from_db, offset, old, flags, out
):
    cz, cx = sz.cz, sz.cx
    lines = low_high(depth, sz.nd, from_da, from_db, (slice(offset, offset + 8), slice(None)))
    strips = low_high(plan, sz.np, from_pa, from_pb, (slice(0, 6 * cz), slice(None)))
    inside = plan > 0, plan < sz.np - 1
    for side in range(2):
        along_z, along_x, along_y = [], [], []
        for c in range(3):
            near = strips[side][c * cz : (c + 1) * cz]
            away = strips[side][(3 + c) * cz : (4 + c) * cz]
            mine = column(sz, velocity, c, 0 if side == 0 else cx - 1)
            line = slice(side * 3 + c, side * 3 + c + 1)
            along_z.append(shifted_rows(near, lines[0][line], lines[1][line]))
            along_x.append(mine - away if side == 0 else away - mine)
            along_y.append(shifted_lanes(near))
        where = lambda c: slice((side * 6 + c) * cz, (side * 6 + c + 1) * cz)
        flag = flags[side * cz : (side + 1) * cz, :]
        got = new_stress(along_z, along_x, along_y, [old[where(c), :] for c in range(6)], flag)
        for c in range(6):
            out[where(c), :] = jnp.where(inside[side], got[c], jnp.zeros_like(got[c]))


def update_stress(
    sz, depth, plan, stress, velocity, flags, from_da, from_db, from_pa, from_pb, out,
    plane_done=None,
):
    cx, cz = sz.cx, sz.cz
    plane = lambda c, z: velocity[c, z * cx : (z + 1) * cx, :]
    d_low, d_high = low_high(
        depth, sz.nd, from_da, from_db, (slice(0, 3 * cx), slice(None))
    )
    p_low, p_high = low_high(plan, sz.np, from_pa, from_pb, (slice(0, 3 * cz), slice(None)))
    for z in range(cz):
        here = slice(z * cx, (z + 1) * cx)
        v = [plane(c, z) for c in range(3)]
        along_z, along_x = [], []
        for c in range(3):
            ahead = plane(c, z + 1) if z + 1 < cz else d_high[c * cx : (c + 1) * cx]
            behind = plane(c, z - 1) if z > 0 else d_low[c * cx : (c + 1) * cx]
            along_z.append(ahead - behind)
            row = slice(c * cz + z, c * cz + z + 1)
            along_x.append(shifted_rows(v[c], p_low[row], p_high[row]))
        along_y = [shifted_lanes(v[c]) for c in range(3)]
        got = new_stress(
            along_z, along_x, along_y, [stress[c, here, :] for c in range(6)], flags[here, :]
        )
        for c in range(6):
            out[c, here, :] = got[c]
        if plane_done is not None:
            plane_done(z)
    return p_low, p_high


def window_from(sz, depth, pile, from_da, from_db, offset):
    def of(c):
        rows = slice(offset + c * sz.pr, offset + (c + 1) * sz.pr)
        low, high = low_high(depth, sz.nd, from_da, from_db, (rows, slice(None)))
        return low, pile[c * sz.pr : (c + 1) * sz.pr, :], high

    return of


def velocity_kernel(sz, step, *refs):
    depth, plan = lax.axis_index("depth"), lax.axis_index("plan")
    take = taker(refs)
    cx, cz = sz.cx, sz.cz
    stress, velocity, density, cell_ids, elem_ids, at_cells, pile = take(7)
    from_da, from_db, from_pa, from_pb = take(4)
    if step > 0:
        old_columns, column_flags, acc = take(3)
    out, to_da, to_db, to_pa, to_pb = take(5)
    if step < STEPS - 1:
        to_all, columns = take(2)
    if step == 0:
        (column_flags,) = take(1)
    if step == STEPS - 1:
        (columns,) = take(1)
    high, low, on_cells = take(3)
    head = 3 * cx
    if step == 0:
        offset = head
        strips = low_high(plan, sz.np, from_pa, from_pb, (slice(0, 7 * cz), slice(None)))
        for side in range(2):
            columns[6 * cz * side : 6 * cz * (side + 1), :] = strips[side][0 : 6 * cz]
            column_flags[cz * side : cz * (side + 1), :] = strips[side][6 * cz :].astype(I32)
    else:
        offset = head + 8
        update_columns(
            sz, depth, plan, velocity, from_pa, from_pb, from_da, from_db, head, old_columns,
            column_flags, columns,
        )
    update_velocity(
        sz, depth, stress, velocity, density, from_da, from_db, columns,
        window_from(sz, depth, pile, from_da, from_db, offset), at_cells, cell_ids, elem_ids,
        out, high, low, on_cells,
    )
    plane = lambda c, z: out[c, z * cx : (z + 1) * cx, :]
    send_layers(sz, depth, range(3), plane, to_da, to_db)
    if step > 0:
        send_sums(sz, depth, 3, acc, to_da, to_db, head)
    shifts = range(2 if step < STEPS - 1 else 1)
    ends = [
        (column(sz, out, c, x), column(sz, out, c, cx - 1 - x)) for x in shifts for c in range(3)
    ]
    send_columns(sz, plan, ends, to_pa, to_pb)
    if step < STEPS - 1:
        store_split(lambda c: out[c], 3, sz.rows, (high, low))
        gather_cells(sz, (high, low), cell_ids, to_all)
        to_pa[6 * cz :, :] = to_all[...]
        to_pb[6 * cz :, :] = to_all[...]


def sums_kernel(sz, step, *refs):
    depth, plan = lax.axis_index("depth"), lax.axis_index("plan")
    take = taker(refs)
    own, from_pa, from_pb = take(3)
    from_others = take(max(sz.np - 3, 0))
    kn, head = sz.kn, 3 * sz.cx
    if step == 0:
        layer_a, layer_b, to_da, to_db, acc, set_ids, sets = take(7)
        sort_sets(sz, plan, own, (from_pa, from_pb, from_others), sets, 4 * kn, 7 * sz.cz)
        for s in range(sz.np):
            ids = sets[s, 3 * kn : 4 * kn, :]
            elem = ids.astype(I32)
            set_ids[s, 0:kn, :] = lax.shift_right_arithmetic(elem, 8)
            set_ids[s, kn : 2 * kn, :] = lax.bitwise_and(elem, COLS - 1)
            sets[s, 3 * kn : 4 * kn, :] = jnp.where(ids >= 0, 1.0, 0.0)
        scatter_sets(sz, 4, sets, set_ids, acc)
        to_da[0:head, :] = layer_a[...]
        to_db[0:head, :] = layer_b[...]
        send_sums(sz, depth, 4, acc, to_da, to_db, head)
    else:
        set_ids, acc, sets = take(3)
        sort_sets(sz, plan, own, (from_pa, from_pb, from_others), sets, 3 * kn, 6 * sz.cz)
        scatter_sets(sz, 3, sets, set_ids, acc)


def stress_kernel(sz, step, *refs):
    depth, plan = lax.axis_index("depth"), lax.axis_index("plan")
    take = taker(refs)
    stress, velocity, flags, from_da, from_db, from_pa, from_pb = take(7)
    pile, mass, jack, acc = take(4)
    cx, cz, head = sz.cx, sz.cz, 3 * sz.cx
    froms = from_da, from_db, from_pa, from_pb
    if step == 0:
        out, to_da, to_db, new_pile, count = take(5)
        count[...] = total_sum(sz, depth, 3, acc, from_da, from_db, head)
    elif step < STEPS - 1:
        count, out, to_da, to_db, new_pile = take(5)
    else:
        count, stress_out, velocity_out, pile_out, out, new_pile, flat_pile, sems = take(8)
        copies = [pltpu.make_async_copy(velocity, velocity_out, sems.at[cz])]
        copies[0].start()
    move_pile(sz, depth, pile, jack, mass, count, acc, from_da, from_db, head, new_pile)
    if step < STEPS - 1:
        strips = update_stress(sz, depth, plan, stress, velocity, flags, *froms, out)
        plane = lambda c, z: out[c, z * cx : (z + 1) * cx, :]
        send_layers(sz, depth, DEPTH_PART, plane, to_da, to_db)
        lines = [
            [strips[side][c * cz + z : c * cz + z + 1] for side in range(2) for c in range(3)]
            for z in (0, cz - 1)
        ]
        blank = [jnp.zeros((2, sz.cy), F32)]
        first, last = [jnp.concatenate(one + blank, axis=0) for one in lines]
        even = depth % 2 == 0
        to_da[head : head + 8, :] = jnp.where(even, last, first)
        to_db[head : head + 8, :] = jnp.where(even, first, last)
        to_da[head + 8 :, :] = new_pile[...]
        to_db[head + 8 :, :] = new_pile[...]
        return
    for r in range(sz.pr):
        for c in range(3):
            row = c * sz.pr + r
            flat_pile[c : c + 1, r * COLS : (r + 1) * COLS] = new_pile[row : row + 1, :]
    copies.append(pltpu.make_async_copy(flat_pile, pile_out, sems.at[cz + 1]))
    copies[-1].start()

    def plane_done(z):
        part = (slice(None), pl.ds(z * cx, cx), slice(None))
        copies.append(pltpu.make_async_copy(out.at[part], stress_out.at[part], sems.at[z]))
        copies[-1].start()

    update_stress(sz, depth, plan, stress, velocity, flags, *froms, out, plane_done)
    for copy in copies:
        copy.wait()


def call(body, ins, outs, scratch=(), copies=0, far_ins=False, far_outs=False, flops=0):
    vmem, far = pl.BlockSpec(memory_space=pltpu.VMEM), pl.BlockSpec(memory_space=pl.ANY)
    sems = [pltpu.SemaphoreType.DMA((copies,))] if copies else []
    moved = sum(4 * x.size for x in ins) + sum(4 * math.prod(shape) for shape, _ in outs)
    return pl.pallas_call(
        body,
        out_shape=[jax.ShapeDtypeStruct(shape, dtype) for shape, dtype in outs],
        in_specs=[far if far_ins else vmem] * len(ins),
        out_specs=[far if far_outs else vmem] * len(outs),
        scratch_shapes=[pltpu.VMEM(shape, dtype) for shape, dtype in scratch] + sems,
        compiler_params=pltpu.CompilerParams(vmem_limit_bytes=48 * 2**20),
        cost_estimate=pl.CostEstimate(flops=flops, bytes_accessed=moved, transcendentals=0),
    )(*[pltpu.with_memory_space_constraint(x, pltpu.HBM) if far_ins else x for x in ins])


def matchings(count):
    first = [(i, i ^ 1) for i in range(count)]
    second = [(i, (i - 1) % count if i % 2 == 0 else (i + 1) % count) for i in range(count)]
    return first, second


def shards(
    stress, velocity, density, flags, pile_velocity, pile_mass, jack_force, pair_elem, pair_cell
):
    sz = Sizes(stress, pile_velocity, pair_cell)
    cz, cx, cy, rows, kn, pr = sz.cz, sz.cx, sz.cy, sz.rows, sz.kn, sz.pr
    assert cy == COLS and sz.pile % COLS == 0 and sz.pairs % COLS == 0
    assert sz.nd % 2 == 0 and sz.np % 2 == 0
    d_first, d_second = matchings(sz.nd)
    p_first, p_second = matchings(sz.np)

    def swap_plan(pa, pb):
        pb = lax.ppermute(pb, "plan", p_second)
        pa = lax.ppermute(pa, "plan", p_first)
        return [pa, pb]

    def swap_depth(da, db):
        db = lax.ppermute(db, "depth", d_second)
        da = lax.ppermute(da, "depth", d_first)
        return [da, db]

    def to_others(x):
        found = []
        for s in range(2, sz.np - 1):
            found.append(
                lax.ppermute(x, "plan", [(i, (i + s) % sz.np) for i in range(sz.np)])
            )
        return found

    full_shape = stress.shape, velocity.shape
    stress = stress.reshape(6, rows, cy)
    velocity = velocity.reshape(3, rows, cy)
    density = density.reshape(rows, cy)
    flags = flags.reshape(rows, cy)
    pr3, wp = 3 * pr, sz.wp
    tables = [((max(3 * rows, 3 * wp), COLS), BF16)] * 2
    cells = [((3 * rows, COLS), F32)]
    scatter = 4 * 3 * wp * COLS * sz.pairs * sz.np
    layers = lambda extra: [((3 * cx + extra, COLS), F32)] * 2
    strips = lambda extra: [((extra, COLS), F32)] * 2

    to = call(
        functools.partial(first_kernel, sz),
        [
            pair_cell, velocity, pair_elem, pile_velocity, pile_mass.reshape(1, -1), jack_force,
            stress, flags, density,
        ],
        layers(pr3)
        + strips(7 * cz + 4 * kn)
        + [
            ((4 * kn, COLS), F32), ((2 * kn, COLS), I32), ((2 * kn, COLS), I32),
            ((pr3, COLS), F32), ((pr, COLS), F32), ((pr3, COLS), F32),
            (stress.shape, F32), (velocity.shape, F32), (density.shape, F32), (flags.shape, I32),
        ],
        tables
        + [(pile_velocity.shape, F32), ((1, sz.pile), F32), (jack_force.shape, F32)]
        + [(pair_elem.shape, I32), (pair_cell.shape, I32)],
        copies=9,
        far_ins=True,
    )
    at_cells, cell_ids, elem_ids, pile, mass, jack = to[4:10]
    stress, velocity, density, flags = to[10:]
    others = to_others(at_cells)
    by_plan = swap_plan(*to[2:4])
    by_depth = swap_depth(*to[0:2])
    count = acc = set_ids = columns = column_flags = None
    for step in range(STEPS):
        last = step == STEPS - 1
        state = [] if step == 0 else [columns, column_flags, acc]
        moved = call(
            functools.partial(velocity_kernel, sz, step),
            [stress, velocity, density, cell_ids, elem_ids, at_cells, pile]
            + by_depth
            + by_plan
            + state,
            [(velocity.shape, F32)]
            + layers(0 if step == 0 else pr3)
            + strips(3 * cz if last else 6 * cz + 3 * kn)
            + ([] if last else [((3 * kn, COLS), F32), ((12 * cz, COLS), F32)])
            + ([((2 * cz, COLS), I32)] if step == 0 else []),
            ([((12 * cz, COLS), F32)] if last else []) + tables + cells,
        )
        velocity, layer = moved[0], list(moved[1:3])
        sets = [at_cells, *by_plan, *others]
        if not last:
            at_cells, columns = moved[5:7]
            others = to_others(at_cells)
        by_plan = swap_plan(*moved[3:5])
        if step == 0:
            column_flags = moved[7]
            *layer, acc, set_ids = call(
                functools.partial(sums_kernel, sz, 0),
                sets + layer,
                layers(4 * pr)
                + [((4 * wp, COLS), F32), ((sz.np, 2 * kn, COLS), I32)],
                [((sz.np, 4 * kn, COLS), F32)],
                flops=scatter,
            )
        by_depth = swap_depth(*layer)
        ins = [stress, velocity, flags, *by_depth, *by_plan, pile, mass, jack, acc]
        ins = ins if step == 0 else ins + [count]
        if last:
            stress, velocity, pile = call(
                functools.partial(stress_kernel, sz, step),
                ins,
                [(stress.shape, F32), (velocity.shape, F32), (pile_velocity.shape, F32)],
                [(stress.shape, F32), ((pr3, COLS), F32), (pile_velocity.shape, F32)],
                copies=cz + 2,
                far_outs=True,
            )
            break
        got = call(
            functools.partial(stress_kernel, sz, step),
            ins,
            [(stress.shape, F32)]
            + layers(8 + pr3)
            + [((pr3, COLS), F32)]
            + ([((pr, COLS), F32)] if step == 0 else []),
        )
        stress, pile = got[0], got[3]
        count = got[4] if step == 0 else count
        by_depth = swap_depth(*got[1:3])
        (acc,) = call(
            functools.partial(sums_kernel, sz, step + 1),
            [at_cells, *by_plan, *others, set_ids],
            [((3 * wp, COLS), F32)],
            [((sz.np, 3 * kn, COLS), F32)],
            flops=scatter,
        )
    return stress.reshape(full_shape[0]), velocity.reshape(full_shape[1]), pile


def solution(mesh):
    cells, field = P("depth", "plan", None), P(None, "depth", "plan", None)
    pile, pairs = P(None, "depth"), P("depth", "plan")
    return jax.shard_map(
        shards,
        mesh=mesh,
        in_specs=(field, field, cells, cells, pile, P("depth"), pile, pairs, pairs),
        out_specs=(field, field, pile),
        check_vma=False,
    )
```
